32 devices in a mesh: atoms: 16 (over z, y, x), bricks: 2 (over core).
Axes of the slice: x: 2, y: 2, z: 4, core: 2. Of those that a mesh axis runs over, the one named last changes fastest.
Arguments:
- orbitals: bfloat16 [32, 32, 32, 32], P('atoms'), may hold values from -6 to 6
- offsets: int32 [32, 3], P('atoms'), may hold values from 0 to 224, as said below
- kernel: float32 [32, 6], P(('atoms', 'bricks')), may hold values from -3 to 3
- pattern: int32 [32, 6], P(('atoms', 'bricks')), may hold values 0 or 1
- local_potential: float32 [512, 64, 256], P('atoms', None, 'bricks'), may hold values from -1 to 1
Outputs:
- density: float32 [512, 64, 256], P('atoms', None, 'bricks')
- gradient: bfloat16 [32, 32, 32, 32], P(('atoms', 'bricks'))
The draws below stay inside these ranges and needn't reach their ends.
Inputs may be any that keep to these rules, and one draw needn't show every extreme that they name: offsets[a,0] lies in 0..31, offsets[a,1] in 0..32, offsets[a,2] in 0..224.
All inputs are finite; a program needn't handle non-finite values. No bound on the sum of `pattern` on one device may be relied on, other than what follows from the above.
Results may differ from the reference program's by a relative error of at most 0.0049.
Values may be sent and summed in bfloat16 or wider, within the bound.
No kernel may reach another device: no remote copies, remote signals or barrier semaphores. Data moves between devices by JAX's collectives and lax.ppermute only.
A program may use at most 64 MiB of HBM per device.

```python
import jax
import jax.numpy as jnp
from jax import lax

B = 32
ORB_ATOM = 2
Y = 64
Z = 256
NORB = 32
NX = 512
N_ATOMS = 16


def draw_offsets(key, part):
    first_key, second_key, third_key = jax.random.split(jax.random.fold_in(key, 7), 3)
    plane = jax.random.randint(first_key, (NORB, 1), 0, B)
    middle = jax.random.randint(second_key, (NORB, 1), 0, Y - B + 1)
    depth = jax.random.randint(third_key, (NORB, 1), 0, Z - B + 1)
    return jnp.concatenate([plane, middle, depth], 1).astype(jnp.int32)


def set_ends(values, own_key, low, largest):
    index_at = [jax.random.randint(jax.random.fold_in(own_key, axis), (), 0, length) for axis, length in enumerate(values.shape)]
    widest = values.shape.index(max(values.shape))
    neighbour = index_at[:widest] + [(index_at[widest] + 1) % values.shape[widest]] + index_at[widest + 1:]
    return values.at[tuple(index_at)].set(low).at[tuple(neighbour)].set(largest)


def block_levels(own_key, dims, cuts, smallest, top_value):
    level = 1.0
    for axis_at, shards_of in cuts:
        heights = jax.random.uniform(jax.random.fold_in(jax.random.fold_in(own_key, 6), axis_at), (shards_of,), jnp.float32, smallest / len(cuts), top_value / len(cuts))
        level = level * jnp.repeat(jnp.exp(heights), dims[axis_at] // shards_of).reshape((-1,) + (1,) * (len(dims) - 1 - axis_at))
    return level


def gaussian(rng, dims, spread, limit, shards=(), kind=jnp.bfloat16):
    array = spread * jax.random.normal(rng, dims, jnp.float32)
    if shards:
        array = array * block_levels(rng, dims, shards, -0.22, 0.18)
    return jnp.clip(array, -limit, limit).astype(kind)


def setup_inputs(seed: int = 0) -> dict:
    keys = jax.random.split(jax.random.key(seed), 6)
    orbitals = gaussian(keys[0], (NORB, B, B, B), 1.0, 6.0, ((0, 16),))
    offsets = draw_offsets(jax.random.fold_in(keys[5], 71), 0)
    kernel = gaussian(keys[2], (NORB, 3 * ORB_ATOM), 0.5, 3.0, ((0, 32),), jnp.float32)
    pattern = set_ends((jax.random.randint(keys[3], (NORB, 3 * ORB_ATOM), 0, 4) < 3).astype(jnp.int32), jax.random.fold_in(keys[3], 1), 0, 1)
    local_potential = jnp.clip(jax.random.uniform(keys[4], (NX, Y, Z), jnp.float32, -1.0, 1.0) * block_levels(keys[4], (NX, Y, Z), ((0, 16), (2, 2)), -0.4, 0.0), -1.0, 1.0)
    return dict(orbitals=orbitals, offsets=offsets, kernel=kernel, pattern=pattern, local_potential=local_potential)


def shifted(orbital, move):
    side = orbital.shape[0]
    cell_index = jnp.arange(side, dtype=jnp.int32)
    result = orbital.astype(jnp.float32)
    for axis_pos in range(3):
        source = cell_index - move[axis_pos]
        inside = ((source >= 0) & (source < side)).astype(jnp.float32)
        source = jnp.clip(source, 0, side - 1).astype(jnp.int32)
        result = jnp.take(result, source, axis=axis_pos)
        layout = [1, 1, 1]
        layout[axis_pos] = side
        result = result * inside.reshape(layout)
    return result

def reference(orbitals, offsets, kernel, pattern, local_potential):
    orbital_count = orbitals.shape[0]
    box_side = orbitals.shape[1]
    weights = kernel * pattern.astype(jnp.float32)
    shell_shift = (jnp.arange(3 * ORB_ATOM, dtype=jnp.int32) // ORB_ATOM - 1) * box_side

    def mix_one(index):
        index = index.astype(jnp.int32)
        domain = index // ORB_ATOM
        partner = jnp.mod((domain - 1) * ORB_ATOM + jnp.arange(3 * ORB_ATOM, dtype=jnp.int32), orbital_count).astype(jnp.int32)
        moves = offsets[partner] - offsets[index][None, :]
        moves = jnp.concatenate([moves[:, :1] + shell_shift[:, None], moves[:, 1:]], 1)
        terms = jax.vmap(shifted)(orbitals[partner], moves)
        return lax.optimization_barrier(jnp.sum(weights[index][:, None, None, None] * terms, 0))
    mixed = lax.map(mix_one, jnp.arange(orbital_count, dtype=jnp.int32))
    grid_x = box_side * N_ATOMS
    products = orbitals.astype(jnp.float32) * mixed
    grid = jnp.zeros((grid_x + box_side, Y, Z), jnp.float32)

    def deposit(index, grid):
        index = jnp.asarray(index).astype(jnp.int32)
        corner = offsets[index]
        start_x = index // ORB_ATOM * box_side + corner[0]
        spot = (start_x, corner[1], corner[2])
        region = lax.dynamic_slice(grid, spot, (box_side, box_side, box_side))
        return lax.dynamic_update_slice(grid, region + products[index], spot)
    grid = lax.fori_loop(0, orbital_count, deposit, grid)
    density = jnp.concatenate([grid[:box_side] + grid[grid_x:], grid[box_side:grid_x]], 0)
    potential = (local_potential + density * lax.rsqrt(1.0 + density * density)).astype(jnp.bfloat16)
    padded = jnp.concatenate([potential, potential[:box_side]], 0)

    def gradient_one(index):
        index = index.astype(jnp.int32)
        corner = offsets[index]
        start_x = index // ORB_ATOM * box_side + corner[0]
        window = lax.dynamic_slice(padded, (start_x, corner[1], corner[2]), (box_side, box_side, box_side))
        return (2.0 * window.astype(jnp.float32) * mixed[index]).astype(jnp.bfloat16)
    gradient = lax.map(gradient_one, jnp.arange(orbital_count, dtype=jnp.int32))
    return (density, gradient)
```

```python
import jax
import jax.numpy as jnp
from jax import lax
from jax.experimental import pallas as pl
from jax.experimental.pallas import tpu as pltpu
from jax.sharding import PartitionSpec as P

LANES = 128
SUB = 8
F32 = jnp.float32
BF16 = jnp.bfloat16
I32 = jnp.int32
VMEM = pl.BlockSpec(memory_space=pltpu.VMEM)
SMEM = pl.BlockSpec(memory_space=pltpu.SMEM)


def iota(shape, dim):
    return lax.broadcasted_iota(I32, shape, dim)


def rows_splat(values, count):
    tiles = []
    for start in range(0, count, SUB):
        tile = jnp.zeros((SUB, LANES), F32)
        row = iota((SUB, LANES), 0)
        for r in range(SUB):
            if start + r < len(values) and values[start + r] is not None:
                tile = jnp.where(row == r, values[start + r], tile)
        tiles.append(tile)
    return jnp.concatenate(tiles, 0)


def pack_kernel(offs, kern, pat, kern_other, pat_other, orbs, out):
    core = lax.axis_index("bricks")
    count, side = orbs.shape[0], orbs.shape[1]
    groups = LANES // side
    per = side // groups
    k_at, lane = iota((side, LANES), 0), iota((side, LANES), 1)
    metas = []
    for rel in range(count):
        orb = jnp.bitwise_xor(core, rel)
        o0, o1, o2 = offs[orb, 0], offs[orb, 1], offs[orb, 2]
        metas += [o0, o1, o2]
        turned = (lane & (side - 1)) == ((k_at + o2) & (side - 1))
        total = jnp.zeros((per * side, LANES), F32)
        for g in range(groups):
            spread = jnp.where(turned & ((lane // side) == g), 1.0, 0.0).astype(BF16)
            planes = [orbs[orb, (g * per + i - o0) & (side - 1)] for i in range(per)]
            total = total + jnp.dot(
                jnp.concatenate(planes, 0), spread, preferred_element_type=F32
            )
        for i in range(per):
            plane = pltpu.roll(total[i * side : (i + 1) * side], o1 & (side - 1), 0)
            out[rel * per + i] = plane.astype(BF16)
    values = [jnp.full((1, LANES), m, I32).astype(F32) for m in metas] + [None] * 2
    for rel in range(count):
        kr, pr = (kern, pat) if rel == 0 else (kern_other, pat_other)
        for c in range(3 * count):
            at = (c // count) * count + jnp.bitwise_xor(core, c % count)
            w = jnp.full((1, LANES), kr[0, at] * pr[0, at].astype(F32), F32)
            high = w.astype(BF16).astype(F32)
            values += [high, w - high]
    out[count * per] = rows_splat(values, side).astype(BF16)


def cut_kernel(offs, offs_prev, v_own, v_other, cut_own, cut_prev):
    core = lax.axis_index("bricks")
    side, depth = v_own.shape[0], v_own.shape[1]
    groups = LANES // side
    per = side // groups
    at = iota((2 * LANES, LANES), 0)
    lane = iota((2 * LANES, LANES), 1)
    z_at = jnp.where(at < LANES, core * LANES + at, (1 - core) * LANES + at - LANES)
    picks = []
    for table in (offs, offs_prev):
        o2 = table[core, 2]
        picks.append(
            jnp.where(z_at == o2 + (((lane & (side - 1)) - o2) & (side - 1)), 1.0, 0.0)
        )
    pick = jnp.concatenate(picks, 1)
    group = (iota((1, 2 * LANES), 1) & (LANES - 1)) // side
    total = jnp.zeros((per * depth, 2 * LANES), F32)
    for g in range(groups):
        here = jnp.where(group == g, 1.0, 0.0)
        left = v_own[g * per : (g + 1) * per].reshape(per * depth, LANES)
        right = v_other[g * per : (g + 1) * per].reshape(per * depth, LANES)
        both = jnp.concatenate([left.astype(BF16), right.astype(BF16)], 1)
        total = total + jnp.dot(both, (pick * here).astype(BF16), preferred_element_type=F32)
    row = iota((side, LANES), 0)
    for t, (table, cut) in enumerate(((offs, cut_own), (offs_prev, cut_prev))):
        o1 = table[core, 1]
        for i in range(per):
            low = total[i * depth : i * depth + side, t * LANES : (t + 1) * LANES]
            high = total[i * depth + depth - side : (i + 1) * depth, t * LANES : (t + 1) * LANES]
            cut[i] = jnp.where(row >= o1, low, high).astype(BF16)


def quadratic(fields, weights):
    total = None
    for a in range(len(fields)):
        inner = None
        for b in range(a, len(fields)):
            if (a, b) in weights:
                term = weights[a, b] * fields[b]
                inner = term if inner is None else inner + term
        total = fields[a] * inner if total is None else total + fields[a] * inner
    return total


def density_kernel(prev, own, following, dens, mixed, bend, placed):
    core = lax.axis_index("bricks")
    side = dens.shape[0]
    groups = LANES // side
    per = side // groups
    packets = (prev, own, following)
    count = (prev.shape[0] - 1) // per
    metas = [packet[count * per].astype(F32) for packet in packets]
    orbs = [(d, o) for d in range(3) for o in range(count)]
    corner = {}
    for d, o in orbs:
        corner[d, o] = [
            metas[d][3 * o + axis : 3 * o + axis + 1].astype(I32) for axis in range(3)
        ]

    def weight(a, b):
        at = SUB + 2 * (orbs[a][1] * 3 * count + (orbs[b][0] - orbs[a][0] + 1) * count + orbs[b][1])
        return metas[orbs[a][0]][at : at + 1] + metas[orbs[a][0]][at + 1 : at + 2]

    pair = {}
    for a in range(len(orbs)):
        for b in range(a, len(orbs)):
            if orbs[b][0] - orbs[a][0] <= 1:
                w = weight(a, b) if a == b else weight(a, b) + weight(b, a)
                pair[a, b] = jnp.broadcast_to(w, (side, LANES))
    wide = groups * LANES
    from_lane, to = iota((LANES, wide), 0), iota((LANES, wide), 1)
    replicate = jnp.where(from_lane == (to // LANES) * side + (to & (side - 1)), 1.0, 0.0).astype(BF16)
    lane = iota((1, LANES), 1)
    to_row = iota((1, wide), 1)
    here = range(2 * count)
    for b in here:
        d, o = orbs[b]
        o0, o1, o2 = corner[d, o]
        z_own = core * LANES + (to_row & (LANES - 1))
        o2w = jnp.concatenate([o2] * groups, 1)
        z_orb = o2w + (((to_row & (side - 1)) - o2w) & (side - 1))
        spread = replicate * jnp.where(z_own == z_orb, 1.0, 0.0).astype(BF16)
        planes = []
        for i in range(per):
            x = (lane // side) * per + i
            keep = (x < o0) if d == 0 else (x >= o0)
            planes.append(packets[d][o * per + i] * jnp.where(keep, 1.0, 0.0).astype(BF16))
        placed[b] = jnp.dot(jnp.concatenate(planes, 0), spread, preferred_element_type=F32)
    row = iota((side, LANES), 0)
    for i in range(per):
        for g in range(groups):
            fields = [placed[b, i * side : (i + 1) * side, g * LANES : (g + 1) * LANES] for b in here]
            halves = []
            for half in range(2):
                cut = []
                for b in here:
                    low = row >= corner[orbs[b]][1]
                    cut.append(jnp.where(low if half == 0 else ~low, fields[b], 0.0))
                halves.append(quadratic(cut, pair))
            x = g * per + i
            dens[x, 0:side] = halves[0]
            dens[x, side : 2 * side] = halves[1]
    me = count
    a0, a1, a2 = corner[orbs[me]]
    z_me = a2 + (((lane & (side - 1)) - a2) & (side - 1))
    for i in range(per):
        x = (lane // side) * per + i
        slab_me = jnp.where(x < a0, 1, 0)
        fields = []
        for b in range(len(orbs)):
            d, o = orbs[b]
            field = packets[d][o * per + i].astype(F32)
            if b != me:
                o0, o1, o2 = corner[d, o]
                slab = jnp.where(x < o0, 1, 0) + (d - 1)
                same = (slab == slab_me) & (o2 + (((lane & (side - 1)) - o2) & (side - 1)) == z_me)
                field = field * jnp.where(same, 1.0, 0.0)
                field = jnp.where((row < o1) == (row < a1), field, 0.0)
            fields.append(field)
        mix = None
        for b in range(len(orbs)):
            term = jnp.broadcast_to(weight(me, b), (side, LANES)) * fields[b]
            mix = term if mix is None else mix + term
        mixed[i] = mix
        rho = quadratic(fields, pair)
        bend[i] = rho * lax.rsqrt(1.0 + rho * rho)


def gradient_kernel(offs, cut_own, cut_next, mixed, bend, out):
    core = lax.axis_index("bricks")
    side = out.shape[1]
    groups = LANES // side
    per = side // groups
    o0, o1, o2 = offs[core, 0], offs[core, 1], offs[core, 2]
    lane = iota((1, LANES), 1)
    planes = []
    for i in range(per):
        x = (lane // side) * per + i
        outer = jnp.where(x < o0, cut_next[i].astype(F32), cut_own[i].astype(F32))
        potential = (outer + bend[i]).astype(BF16).astype(F32)
        grad = 2.0 * potential * mixed[i]
        planes.append(pltpu.roll(grad, (side - o1) & (side - 1), 0).astype(BF16))
    stacked = jnp.concatenate(planes, 0)
    from_lane, k_at = iota((LANES, side), 0), iota((LANES, side), 1)
    turned = (from_lane & (side - 1)) == ((k_at + o2) & (side - 1))
    for g in range(groups):
        gather = jnp.where(turned & ((from_lane // side) == g), 1.0, 0.0).astype(BF16)
        part = jnp.dot(stacked, gather, preferred_element_type=F32).astype(BF16)
        for i in range(per):
            out[0, (g * per + i - o0) & (side - 1)] = part[i * side : (i + 1) * side]


def call(kernel, name, outs, ins, args, scratch=()):
    return pl.pallas_call(
        kernel,
        name=name,
        out_shape=outs,
        in_specs=ins,
        out_specs=jax.tree.map(lambda _: VMEM, outs),
        scratch_shapes=scratch,
        cost_estimate=pl.CostEstimate(flops=1000000, bytes_accessed=2000000, transcendentals=0),
    )(*args)


def local(orbitals, offsets, kernel, pattern, local_potential):
    devices = lax.axis_size("atoms")
    up = [(i, (i + 1) % devices) for i in range(devices)]
    down = [(j, i) for i, j in up]
    swap = [(0, 1), (1, 0)]
    count, side = orbitals.shape[0], orbitals.shape[1]
    depth, width = local_potential.shape[1], local_potential.shape[2]
    per = side * side // LANES
    shape = jax.ShapeDtypeStruct
    offsets_prev = lax.ppermute(offsets, "atoms", up)
    other = lax.ppermute(local_potential, "bricks", swap)
    kernel_other = lax.ppermute(kernel, "bricks", swap)
    pattern_other = lax.ppermute(pattern, "bricks", swap)
    packet = call(
        pack_kernel,
        "pack",
        shape((count * per + 1, side, LANES), BF16),
        [SMEM] * 5 + [VMEM],
        (offsets, kernel, pattern, kernel_other, pattern_other, orbitals),
    )
    prev = lax.ppermute(packet, "atoms", up)
    following = lax.ppermute(packet, "atoms", down)
    cut_own, cut_prev = call(
        cut_kernel,
        "cut",
        (shape((per, side, LANES), BF16),) * 2,
        [SMEM] * 2 + [VMEM] * 2,
        (offsets, offsets_prev, local_potential, other),
    )
    cut_next = lax.ppermute(cut_prev, "atoms", down)
    density, mixed, bend = call(
        density_kernel,
        "density",
        (
            shape((side, depth, width), F32),
            shape((per, side, LANES), F32),
            shape((per, side, LANES), F32),
        ),
        [VMEM] * 3,
        (prev, packet, following),
        [pltpu.VMEM((2 * count, per * side, LANES // side * LANES), F32)],
    )
    gradient = call(
        gradient_kernel,
        "gradient",
        shape((1, side, side, side), BF16),
        [SMEM] + [VMEM] * 4,
        (offsets, cut_own, cut_next, mixed, bend),
    )
    return density, gradient


def solution(mesh):
    return jax.shard_map(
        local,
        mesh=mesh,
        in_specs=(
            P("atoms", None, None, None),
            P("atoms", None),
            P(("atoms", "bricks"), None),
            P(("atoms", "bricks"), None),
            P("atoms", None, "bricks"),
        ),
        out_specs=(P("atoms", None, "bricks"), P(("atoms", "bricks"), None, None, None)),
        check_vma=False,
    )
```

```python
import jax
import jax.numpy as jnp
from jax import lax
from jax.experimental import pallas as pl
from jax.experimental.pallas import tpu as pltpu
from jax.sharding import PartitionSpec as P

LANES = 128
SUB = 8
F32 = jnp.float32
BF16 = jnp.bfloat16
I32 = jnp.int32
VMEM = pl.BlockSpec(memory_space=pltpu.VMEM)
HBM = pl.BlockSpec(memory_space=pltpu.HBM)
GRANT = 16 * 2**20


def iota(shape, dim):
    return lax.broadcasted_iota(I32, shape, dim)


def rows_splat(values, count):
    tiles = []
    for start in range(0, count, SUB):
        tile = jnp.zeros((SUB, LANES), F32)
        row = iota((SUB, LANES), 0)
        for r in range(SUB):
            if start + r < len(values) and values[start + r] is not None:
                tile = jnp.where(row == r, values[start + r], tile)
        tiles.append(tile)
    return jnp.concatenate(tiles, 0)


def pack_kernel(offs_hbm, kern_hbm, pat_hbm, kern_other, pat_other, orbs_hbm, out, offs, kern, pat, orbs, sems):
    copies = [
        pltpu.make_async_copy(src, dst, sems.at[n])
        for n, (src, dst) in enumerate(
            ((offs_hbm, offs), (kern_hbm, kern), (pat_hbm, pat), (orbs_hbm, orbs))
        )
    ]
    for copy in copies:
        copy.start()
    core = lax.axis_index("bricks")
    count, side = orbs.shape[0], orbs.shape[1]
    groups = LANES // side
    per = side // groups
    k_at, lane = iota((side, LANES), 0), iota((side, LANES), 1)
    for copy in copies:
        copy.wait()
    metas = []
    for rel in range(count):
        orb = jnp.bitwise_xor(core, rel)
        o0, o1, o2 = offs[orb, 0], offs[orb, 1], offs[orb, 2]
        metas += [o0, o1, o2]
        turned = (lane & (side - 1)) == ((k_at + o2) & (side - 1))
        total = jnp.zeros((per * side, LANES), F32)
        for g in range(groups):
            spread = jnp.where(turned & ((lane // side) == g), 1.0, 0.0).astype(BF16)
            planes = [orbs[orb, (g * per + i - o0) & (side - 1)] for i in range(per)]
            total = total + jnp.dot(
                jnp.concatenate(planes, 0), spread, preferred_element_type=F32
            )
        for i in range(per):
            plane = pltpu.roll(total[i * side : (i + 1) * side], o1 & (side - 1), 0)
            out[rel * per + i] = plane.astype(BF16)
    values = [jnp.full((1, LANES), m, I32).astype(F32) for m in metas] + [None] * 2
    for rel in range(count):
        kr, pr = (kern, pat) if rel == 0 else (kern_other, pat_other)
        line = kr[...] * pr[...].astype(F32)
        spread = [jnp.broadcast_to(line[:, c : c + 1], (1, LANES)) for c in range(3 * count)]
        for c in range(3 * count):
            w = jnp.where(core == 0, spread[c], spread[c ^ 1])
            high = w.astype(BF16).astype(F32)
            values += [high, w - high]
    out[count * per] = rows_splat(values, side).astype(BF16)


def cut_kernel(packet, offs_prev, v_hbm, v_other, cut_own, cut_prev, v_own, sems):
    side, depth = v_own.shape[0], v_own.shape[1]
    groups = LANES // side
    per = side // groups
    copies = [
        pltpu.make_async_copy(
            v_hbm.at[pl.ds(g * per, per)], v_own.at[pl.ds(g * per, per)], sems.at[g]
        )
        for g in range(groups)
    ]
    for copy in copies:
        copy.start()
    core = lax.axis_index("bricks")
    meta = packet[packet.shape[0] - 1].astype(F32)
    line = jnp.where(core == 0, offs_prev[0:1, :], offs_prev[1:2, :])
    corners = [
        [meta[axis : axis + 1].astype(I32) for axis in range(3)],
        [jnp.broadcast_to(line[:, axis : axis + 1], (1, LANES)) for axis in range(3)],
    ]
    at = iota((2 * LANES, LANES), 0)
    lane = iota((1, LANES), 1)
    z_at = jnp.where(at < LANES, core * LANES + at, (1 - core) * LANES + at - LANES)
    picks = []
    for _, _, o2 in corners:
        picks.append(jnp.where(z_at == o2 + ((lane - o2) & (side - 1)), 1.0, 0.0))
    pick = jnp.concatenate(picks, 1)
    group = (iota((1, 2 * LANES), 1) & (LANES - 1)) // side
    total = jnp.zeros((per * depth, 2 * LANES), F32)
    for g in range(groups):
        here = jnp.where(group == g, 1.0, 0.0)
        copies[g].wait()
        left = v_own[g * per : (g + 1) * per].reshape(per * depth, LANES)
        right = v_other[g * per : (g + 1) * per].reshape(per * depth, LANES)
        both = jnp.concatenate([left.astype(BF16), right.astype(BF16)], 1)
        total = total + jnp.dot(both, (pick * here).astype(BF16), preferred_element_type=F32)
    row = iota((side, LANES), 0)
    for t, cut in enumerate((cut_own, cut_prev)):
        o1 = corners[t][1]
        for i in range(per):
            low = total[i * depth : i * depth + side, t * LANES : (t + 1) * LANES]
            high = total[i * depth + depth - side : (i + 1) * depth, t * LANES : (t + 1) * LANES]
            cut[i] = jnp.where(row >= o1, low, high).astype(BF16)


def quadratic(fields, weights):
    total = None
    for a in range(len(fields)):
        inner = None
        for b in range(a, len(fields)):
            if (a, b) in weights:
                term = weights[a, b] * fields[b]
                inner = term if inner is None else inner + term
        total = fields[a] * inner if total is None else total + fields[a] * inner
    return total


class Tables:
    def __init__(self, packets, per):
        self.count = (packets[0].shape[0] - 1) // per
        self.metas = [packet[self.count * per].astype(F32) for packet in packets]
        self.orbs = [(d, o) for d in range(len(packets)) for o in range(self.count)]
        self.corner = [
            [self.metas[d][3 * o + axis : 3 * o + axis + 1].astype(I32) for axis in range(3)]
            for d, o in self.orbs
        ]

    def weight(self, a, b):
        (da, oa), (db, ob) = self.orbs[a], self.orbs[b]
        at = SUB + 2 * (oa * 3 * self.count + (db - da + 1) * self.count + ob)
        return self.metas[da][at : at + 1] + self.metas[da][at + 1 : at + 2]

    def pairs(self, side):
        pair = {}
        for a in range(len(self.orbs)):
            for b in range(a, len(self.orbs)):
                if self.orbs[b][0] - self.orbs[a][0] <= 1:
                    w = self.weight(a, b)
                    if a != b:
                        w = w + self.weight(b, a)
                    pair[a, b] = jnp.broadcast_to(w, (side, LANES))
        return pair


def brick_kernel(prev, own, dens_hbm, dens, placed, sems):
    core = lax.axis_index("bricks")
    side = dens.shape[0]
    groups = LANES // side
    per = side // groups
    packets = (prev, own)
    tables = Tables(packets, per)
    pair = tables.pairs(side)
    wide = groups * LANES
    from_lane, to = iota((LANES, wide), 0), iota((LANES, wide), 1)
    replicate = jnp.where(from_lane == (to // LANES) * side + (to & (side - 1)), 1.0, 0.0).astype(BF16)
    lane = iota((1, LANES), 1)
    to_row = iota((1, wide), 1)
    z_own = core * LANES + (to_row & (LANES - 1))
    here = range(len(tables.orbs))
    for b in here:
        d, o = tables.orbs[b]
        o0, _, o2 = tables.corner[b]
        o2w = jnp.concatenate([o2] * groups, 1)
        z_orb = o2w + ((to_row - o2w) & (side - 1))
        spread = replicate * jnp.where(z_own == z_orb, 1.0, 0.0).astype(BF16)
        planes = []
        for i in range(per):
            x = (lane // side) * per + i
            keep = (x < o0) if d == 0 else (x >= o0)
            planes.append(packets[d][o * per + i] * jnp.where(keep, 1.0, 0.0).astype(BF16))
        placed[b] = jnp.dot(jnp.concatenate(planes, 0), spread, preferred_element_type=F32)
    row = iota((side, LANES), 0)
    copies = []
    for g in range(groups):
        for i in range(per):
            fields = [placed[b, i * side : (i + 1) * side, g * LANES : (g + 1) * LANES] for b in here]
            x = g * per + i
            for half in range(2):
                cut = []
                for b in here:
                    low = row >= tables.corner[b][1]
                    cut.append(jnp.where(low if half == 0 else ~low, fields[b], 0.0))
                dens[x, half * side : (half + 1) * side] = quadratic(cut, pair)
        copies.append(
            pltpu.make_async_copy(
                dens.at[pl.ds(g * per, per)], dens_hbm.at[pl.ds(g * per, per)], sems.at[g]
            )
        )
        copies[-1].start()
    for copy in copies:
        copy.wait()


def box_kernel(offs_hbm, prev, own, following, cut_own, cut_next, out, offs, sem):
    copy = pltpu.make_async_copy(offs_hbm, offs, sem)
    copy.start()
    core = lax.axis_index("bricks")
    side = out.shape[1]
    groups = LANES // side
    per = side // groups
    packets = (prev, own, following)
    tables = Tables(packets, per)
    me = tables.count
    pair = tables.pairs(side)
    mine = [jnp.broadcast_to(tables.weight(me, b), (side, LANES)) for b in range(len(tables.orbs))]
    lane = iota((1, LANES), 1)
    row = iota((side, LANES), 0)
    a0, a1, a2 = tables.corner[me]
    z_me = a2 + ((lane - a2) & (side - 1))
    copy.wait()
    s0, s1, s2 = offs[core, 0], offs[core, 1], offs[core, 2]
    planes = []
    for i in range(per):
        x = (lane // side) * per + i
        slab_me = jnp.where(x < a0, 1, 0)
        fields = []
        for b, (d, o) in enumerate(tables.orbs):
            field = packets[d][o * per + i].astype(F32)
            if b != me:
                o0, o1, o2 = tables.corner[b]
                slab = jnp.where(x < o0, 1, 0) + (d - 1)
                same = (slab == slab_me) & (o2 + ((lane - o2) & (side - 1)) == z_me)
                field = field * jnp.where(same, 1.0, 0.0)
                field = jnp.where((row < o1) == (row < a1), field, 0.0)
            fields.append(field)
        mix = None
        for b in range(len(fields)):
            term = mine[b] * fields[b]
            mix = term if mix is None else mix + term
        rho = quadratic(fields, pair)
        bend = rho * lax.rsqrt(1.0 + rho * rho)
        outer = jnp.where(x < a0, cut_next[i].astype(F32), cut_own[i].astype(F32))
        potential = (outer + bend).astype(BF16).astype(F32)
        grad = 2.0 * potential * mix
        planes.append(pltpu.roll(grad, (side - s1) & (side - 1), 0).astype(BF16))
    stacked = jnp.concatenate(planes, 0)
    from_lane, k_at = iota((LANES, side), 0), iota((LANES, side), 1)
    turned = (from_lane & (side - 1)) == ((k_at + s2) & (side - 1))
    for g in range(groups):
        gather = jnp.where(turned & ((from_lane // side) == g), 1.0, 0.0).astype(BF16)
        part = jnp.dot(stacked, gather, preferred_element_type=F32).astype(BF16)
        for i in range(per):
            out[0, (g * per + i - s0) & (side - 1)] = part[i * side : (i + 1) * side]


def call(kernel, outs, out_specs, ins, args, scratch):
    return pl.pallas_call(
        kernel,
        out_shape=outs,
        in_specs=ins,
        out_specs=out_specs,
        scratch_shapes=scratch,
        compiler_params=pltpu.CompilerParams(vmem_limit_bytes=GRANT),
        cost_estimate=pl.CostEstimate(
            flops=1000000, bytes_accessed=2000000, transcendentals=0
        ),
    )(*[
        pltpu.with_memory_space_constraint(x, pltpu.HBM) if spec is HBM else x
        for x, spec in zip(args, ins)
    ])


def step(orbitals, offsets, kernel, pattern, local_potential):
    devices = lax.axis_size("atoms")
    up = [(i, (i + 1) % devices) for i in range(devices)]
    down = [(j, i) for i, j in up]
    swap = [(0, 1), (1, 0)]
    count, side = orbitals.shape[0], orbitals.shape[1]
    depth, width = local_potential.shape[1], local_potential.shape[2]
    groups = LANES // side
    per = side // groups
    shape = jax.ShapeDtypeStruct
    dma = pltpu.SemaphoreType.DMA
    offsets_prev = lax.ppermute(offsets, "atoms", up)
    kernel_other = lax.ppermute(kernel, "bricks", swap)
    pattern_other = lax.ppermute(pattern, "bricks", swap)
    other = lax.ppermute(local_potential, "bricks", swap)
    packet = call(
        pack_kernel,
        shape((count * per + 1, side, LANES), BF16),
        VMEM,
        [HBM] * 3 + [VMEM] * 2 + [HBM],
        (offsets, kernel, pattern, kernel_other, pattern_other, orbitals),
        [
            pltpu.SMEM(offsets.shape, I32),
            pltpu.VMEM(kernel.shape, F32),
            pltpu.VMEM(pattern.shape, I32),
            pltpu.VMEM(orbitals.shape, BF16),
            dma((4,)),
        ],
    )
    prev = lax.ppermute(packet, "atoms", up)
    following = lax.ppermute(packet, "atoms", down)
    cut_own, cut_prev = call(
        cut_kernel,
        (shape((per, side, LANES), BF16),) * 2,
        (VMEM,) * 2,
        [VMEM] * 2 + [HBM] + [VMEM],
        (packet, offsets_prev, local_potential, other),
        [pltpu.VMEM(local_potential.shape, F32), dma((groups,))],
    )
    cut_next = lax.ppermute(cut_prev, "atoms", down)
    density = call(
        brick_kernel,
        shape((side, depth, width), F32),
        HBM,
        [VMEM] * 2,
        (prev, packet),
        [
            pltpu.VMEM((side, depth, width), F32),
            pltpu.VMEM((2 * count, per * side, groups * LANES), F32),
            dma((groups,)),
        ],
    )
    gradient = call(
        box_kernel,
        shape((1, side, side, side), BF16),
        VMEM,
        [HBM] + [VMEM] * 5,
        (offsets, prev, packet, following, cut_own, cut_next),
        [pltpu.SMEM(offsets.shape, I32), dma(())],
    )
    return density, gradient


def solution(mesh):
    return jax.shard_map(
        step,
        mesh=mesh,
        in_specs=(
            P("atoms", None, None, None),
            P("atoms", None),
            P(("atoms", "bricks"), None),
            P(("atoms", "bricks"), None),
            P("atoms", None, "bricks"),
        ),
        out_specs=(P("atoms", None, "bricks"), P(("atoms", "bricks"), None, None, None)),
        check_vma=False,
    )
```

```python
import jax
import jax.numpy as jnp
from jax import lax
from jax.experimental import pallas as pl
from jax.experimental.pallas import tpu as pltpu
from jax.sharding import PartitionSpec as P

LANES = 128
SUB = 8
F32 = jnp.float32
BF16 = jnp.bfloat16
I32 = jnp.int32
VMEM = pl.BlockSpec(memory_space=pltpu.VMEM)
HBM = pl.BlockSpec(memory_space=pltpu.HBM)
GRANT = 16 * 2**20


def iota(shape, dim):
    return lax.broadcasted_iota(I32, shape, dim)


def rows_splat(values, count):
    tiles = []
    for start in range(0, count, SUB):
        tile = jnp.zeros((SUB, LANES), F32)
        row = iota((SUB, LANES), 0)
        for r in range(SUB):
            if start + r < len(values) and values[start + r] is not None:
                tile = jnp.where(row == r, values[start + r], tile)
        tiles.append(tile)
    return jnp.concatenate(tiles, 0)


def pack_kernel(offs_hbm, kern_hbm, pat_hbm, orbs_hbm, out, offs, kern, pat, orb, sems):
    core = lax.axis_index("bricks")
    copies = [
        pltpu.make_async_copy(src, dst, sems.at[n])
        for n, (src, dst) in enumerate(
            ((offs_hbm, offs), (kern_hbm, kern), (pat_hbm, pat), (orbs_hbm.at[core], orb))
        )
    ]
    for copy in copies:
        copy.start()
    count, side = orbs_hbm.shape[0], orb.shape[0]
    groups = LANES // side
    per = side // groups
    k_at, lane = iota((side, LANES), 0), iota((side, LANES), 1)
    for copy in copies:
        copy.wait()
    corner = [offs[core, axis] for axis in range(3)]
    o0, o1, o2 = corner
    turned = (lane & (side - 1)) == ((k_at + o2) & (side - 1))
    total = jnp.zeros((per * side, LANES), F32)
    for g in range(groups):
        spread = jnp.where(turned & ((lane // side) == g), 1.0, 0.0).astype(BF16)
        planes = [orb[(g * per + i - o0) & (side - 1)] for i in range(per)]
        total = total + jnp.dot(jnp.concatenate(planes, 0), spread, preferred_element_type=F32)
    for i in range(per):
        plane = pltpu.roll(total[i * side : (i + 1) * side], o1 & (side - 1), 0)
        out[i] = plane.astype(BF16)
    values = [jnp.full((1, LANES), m, I32).astype(F32) for m in corner] + [None] * (SUB - 3)
    line = kern[...] * pat[...].astype(F32)
    spread = [jnp.broadcast_to(line[:, c : c + 1], (1, LANES)) for c in range(3 * count)]
    for c in range(3 * count):
        w = jnp.where(core == 0, spread[c], spread[c ^ 1])
        high = w.astype(BF16).astype(F32)
        values += [high, w - high]
    out[per] = rows_splat(values, side).astype(BF16)


def cut_kernel(packet, offs_prev, v_hbm, v_other, cut_own, cut_prev, v_own, sems):
    side, depth = v_own.shape[0], v_own.shape[1]
    groups = LANES // side
    per = side // groups
    copies = [
        pltpu.make_async_copy(
            v_hbm.at[pl.ds(g * per, per)], v_own.at[pl.ds(g * per, per)], sems.at[g]
        )
        for g in range(groups)
    ]
    for copy in copies:
        copy.start()
    core = lax.axis_index("bricks")
    meta = packet[packet.shape[0] - 1].astype(F32)
    line = jnp.where(core == 0, offs_prev[0:1, :], offs_prev[1:2, :])
    corners = [
        [meta[axis : axis + 1].astype(I32) for axis in range(3)],
        [jnp.broadcast_to(line[:, axis : axis + 1], (1, LANES)) for axis in range(3)],
    ]
    at = iota((2 * LANES, LANES), 0)
    lane = iota((1, LANES), 1)
    z_at = jnp.where(at < LANES, core * LANES + at, (1 - core) * LANES + at - LANES)
    picks = []
    for _, _, o2 in corners:
        picks.append(jnp.where(z_at == o2 + ((lane - o2) & (side - 1)), 1.0, 0.0))
    pick = jnp.concatenate(picks, 1)
    group = (iota((1, 2 * LANES), 1) & (LANES - 1)) // side
    total = jnp.zeros((per * depth, 2 * LANES), F32)
    for g in range(groups):
        here = jnp.where(group == g, 1.0, 0.0)
        copies[g].wait()
        left = v_own[g * per : (g + 1) * per].reshape(per * depth, LANES)
        right = v_other[g * per : (g + 1) * per].reshape(per * depth, LANES)
        both = jnp.concatenate([left.astype(BF16), right.astype(BF16)], 1)
        total = total + jnp.dot(both, (pick * here).astype(BF16), preferred_element_type=F32)
    row = iota((side, LANES), 0)
    for t, cut in enumerate((cut_own, cut_prev)):
        o1 = corners[t][1]
        for i in range(per):
            low = total[i * depth : i * depth + side, t * LANES : (t + 1) * LANES]
            high = total[i * depth + depth - side : (i + 1) * depth, t * LANES : (t + 1) * LANES]
            cut[i] = jnp.where(row >= o1, low, high).astype(BF16)


class Tables:
    def __init__(self, packets, places):
        self.places = places
        self.metas = [packet[packet.shape[0] - 1].astype(F32) for packet in packets]
        self.corner = [
            [meta[axis : axis + 1].astype(I32) for axis in range(3)] for meta in self.metas
        ]

    def weight(self, a, b):
        (da, oa), (db, ob) = self.places[a], self.places[b]
        at = SUB + 2 * ((db - da + 1) * 2 + (oa ^ ob))
        return self.metas[a][at : at + 1] + self.metas[a][at + 1 : at + 2]

    def pair(self, a, b):
        return self.weight(a, b) if a == b else self.weight(a, b) + self.weight(b, a)


def brick_kernel(prev0, prev1, own0, own1, dens_hbm, dens, ready, placed, sems):
    core = lax.axis_index("bricks")
    side = dens.shape[0]
    groups = LANES // side
    per = side // groups
    packets = (prev0, prev1, own0, own1)
    many = len(packets)
    tables = Tables(packets, ((0, 0), (0, 1), (1, 0), (1, 1)))
    lane = iota((1, LANES), 1)
    k_at = lane & (side - 1)
    row = iota((side, LANES), 0)
    uppers = [row < tables.corner[b][1] for b in range(many)]
    z_at = [o2 + ((k_at - o2) & (side - 1)) for _, _, o2 in tables.corner]
    links = {}
    for a in range(many):
        for b in range(a, many):
            w = tables.pair(a, b)
            if a != b:
                w = jnp.where(uppers[a] == uppers[b], jnp.where(z_at[a] == z_at[b], w, 0.0), 0.0)
            links[a, b] = jnp.broadcast_to(w, (side, LANES))
    for i in range(per):
        x = (lane // side) * per + i
        fields = []
        for b in range(many):
            o0 = tables.corner[b][0]
            keep = (x < o0) if b < 2 else (x >= o0)
            kept = packets[b][i] * jnp.where(keep, 1.0, 0.0).astype(BF16)
            fields.append(kept.astype(F32))
        for a in range(many):
            inner = links[a, a] * fields[a]
            for b in range(a + 1, many):
                inner = inner + links[a, b] * fields[b]
            product = fields[a] * inner
            high = product.astype(BF16)
            ready[a, i * side : (i + 1) * side, 0:LANES] = high
            ready[a, i * side : (i + 1) * side, LANES:] = (product - high.astype(F32)).astype(BF16)
    wide = groups * LANES
    to = iota((LANES, wide), 1)
    from_lane = iota((LANES, wide), 0)
    spread = jnp.where(from_lane == (to // LANES) * side + (to & (side - 1)), 1.0, 0.0).astype(BF16)
    for a in range(many):
        inside = jnp.where(z_at[a] == core * LANES + lane, 1.0, 0.0).astype(BF16)
        place = spread * jnp.concatenate([inside] * groups, 1)
        out = jnp.dot(ready[a], jnp.concatenate([place] * 2, 0), preferred_element_type=F32)
        placed[a] = out
    copies = []
    for g in range(groups):
        for i in range(per):
            x = g * per + i
            parts = [placed[a, i * side : (i + 1) * side, g * LANES : (g + 1) * LANES] for a in range(many)]
            low, high = None, None
            for a in range(many):
                down = jnp.where(uppers[a], 0.0, parts[a])
                up = jnp.where(uppers[a], parts[a], 0.0)
                low = down if low is None else low + down
                high = up if high is None else high + up
            dens[x, 0:side] = low
            dens[x, side : 2 * side] = high
        copies.append(
            pltpu.make_async_copy(
                dens.at[pl.ds(g * per, per)], dens_hbm.at[pl.ds(g * per, per)], sems.at[g]
            )
        )
        copies[-1].start()
    for copy in copies:
        copy.wait()


def box_kernel(
    offs_hbm, prev0, prev1, own0, own1, next0, next1, cut_own, cut_next, out, offs, grads, sem
):
    copy = pltpu.make_async_copy(offs_hbm, offs, sem)
    copy.start()
    core = lax.axis_index("bricks")
    side = out.shape[1]
    groups = LANES // side
    per = side // groups
    packets = (prev0, prev1, own0, own1, next0, next1)
    tables = Tables(packets, ((0, 0), (0, 1), (1, 0), (1, 1), (2, 0), (2, 1)))
    me, mate = 2, 3
    lane = iota((1, LANES), 1)
    k_at = lane & (side - 1)
    row = iota((side, LANES), 0)
    a0, a1, a2 = tables.corner[me]
    z_me = a2 + ((k_at - a2) & (side - 1))
    upper = row < a1

    def same_yz(b):
        _, o1, o2 = tables.corner[b]
        z = jnp.where(o2 + ((k_at - o2) & (side - 1)) == z_me, 1.0, 0.0)
        return jnp.where((row < o1) == upper, z, 0.0)

    overlap = [None if b == me else same_yz(b) for b in range(6)]
    inner_ids, last_ids = (0, 1, me, mate), (4, 5, me, mate)
    pair = {}
    for a in range(4):
        for b in range(a, 4):
            pair[a, b] = (
                tables.pair(inner_ids[a], inner_ids[b]), tables.pair(last_ids[a], last_ids[b])
            )
    mine = [(tables.weight(me, inner_ids[b]), tables.weight(me, last_ids[b])) for b in range(4)]
    for i in range(per):
        x = (lane // side) * per + i
        spill = x < a0

        def pick(both, a, b):
            return both[0] if a >= 2 and b >= 2 else jnp.where(spill, both[1], both[0])

        fields = []
        for o in (0, 1):
            before = jnp.where((x < tables.corner[o][0]) & ~spill, 1.0, 0.0).astype(BF16)
            after = jnp.where((x >= tables.corner[4 + o][0]) & spill, 1.0, 0.0).astype(BF16)
            fields.append(
                (packets[o][i] * before).astype(F32) * overlap[o]
                + (packets[4 + o][i] * after).astype(F32) * overlap[4 + o]
            )
        fields.append(packets[me][i].astype(F32))
        also = jnp.where((x < tables.corner[mate][0]) == spill, 1.0, 0.0).astype(BF16)
        fields.append((packets[mate][i] * also).astype(F32) * overlap[mate])
        rho = None
        for a in range(4):
            inner = None
            for b in range(a, 4):
                term = pick(pair[a, b], a, b) * fields[b]
                inner = term if inner is None else inner + term
            rho = fields[a] * inner if rho is None else rho + fields[a] * inner
        mix = None
        for b in range(4):
            term = pick(mine[b], b, me) * fields[b]
            mix = term if mix is None else mix + term
        bend = rho * lax.rsqrt(1.0 + rho * rho)
        outer = jnp.where(spill, cut_next[i].astype(F32), cut_own[i].astype(F32))
        potential = (outer + bend).astype(BF16).astype(F32)
        grads[i] = 2.0 * potential * mix
    copy.wait()
    s0, s1, s2 = offs[core, 0], offs[core, 1], offs[core, 2]
    planes = [pltpu.roll(grads[i], (side - s1) & (side - 1), 0).astype(BF16) for i in range(per)]
    stacked = jnp.concatenate(planes, 0)
    from_lane, to = iota((LANES, side), 0), iota((LANES, side), 1)
    turned = (from_lane & (side - 1)) == ((to + s2) & (side - 1))
    for g in range(groups):
        gather = jnp.where(turned & ((from_lane // side) == g), 1.0, 0.0).astype(BF16)
        part = jnp.dot(stacked, gather, preferred_element_type=F32).astype(BF16)
        for i in range(per):
            out[0, (g * per + i - s0) & (side - 1)] = part[i * side : (i + 1) * side]


def call(kernel, outs, out_specs, ins, args, scratch):
    return pl.pallas_call(
        kernel,
        out_shape=outs,
        in_specs=ins,
        out_specs=out_specs,
        scratch_shapes=scratch,
        compiler_params=pltpu.CompilerParams(vmem_limit_bytes=GRANT),
        cost_estimate=pl.CostEstimate(
            flops=1000000, bytes_accessed=2000000, transcendentals=0
        ),
    )(*[
        pltpu.with_memory_space_constraint(x, pltpu.HBM) if spec is HBM else x
        for x, spec in zip(args, ins)
    ])


def step(orbitals, offsets, kernel, pattern, local_potential):
    devices = lax.axis_size("atoms")
    up = [(i, (i + 1) % devices) for i in range(devices)]
    down = [(j, i) for i, j in up]
    swap = [(0, 1), (1, 0)]
    count, side = orbitals.shape[0], orbitals.shape[1]
    depth, width = local_potential.shape[1], local_potential.shape[2]
    groups = LANES // side
    per = side // groups
    shape = jax.ShapeDtypeStruct
    dma = pltpu.SemaphoreType.DMA
    offsets_prev = lax.ppermute(offsets, "atoms", up)
    own = call(
        pack_kernel,
        shape((per + 1, side, LANES), BF16),
        VMEM,
        [HBM] * 4,
        (offsets, kernel, pattern, orbitals),
        [
            pltpu.SMEM(offsets.shape, I32),
            pltpu.VMEM(kernel.shape, F32),
            pltpu.VMEM(pattern.shape, I32),
            pltpu.VMEM(orbitals.shape[1:], BF16),
            dma((4,)),
        ],
    )
    prev = lax.ppermute(own, "atoms", up)
    following = lax.ppermute(own, "atoms", down)
    other = lax.ppermute(local_potential, "bricks", swap)
    own_mate = lax.ppermute(own, "bricks", swap)
    cut_own, cut_prev = call(
        cut_kernel,
        (shape((per, side, LANES), BF16),) * 2,
        (VMEM,) * 2,
        [VMEM] * 2 + [HBM] + [VMEM],
        (own, offsets_prev, local_potential, other),
        [pltpu.VMEM(local_potential.shape, F32), dma((groups,))],
    )
    cut_next = lax.ppermute(cut_prev, "atoms", down)
    prev_mate = lax.ppermute(prev, "bricks", swap)
    following_mate = lax.ppermute(following, "bricks", swap)
    density = call(
        brick_kernel,
        shape((side, depth, width), F32),
        HBM,
        [VMEM] * 4,
        (prev, prev_mate, own, own_mate),
        [
            pltpu.VMEM((side, depth, width), F32),
            pltpu.VMEM((2 * count, per * side, 2 * LANES), BF16),
            pltpu.VMEM((2 * count, per * side, groups * LANES), F32),
            dma((groups,)),
        ],
    )
    gradient = call(
        box_kernel,
        shape((1, side, side, side), BF16),
        VMEM,
        [HBM] + [VMEM] * 8,
        (
            offsets,
            prev,
            prev_mate,
            own,
            own_mate,
            following,
            following_mate,
            cut_own,
            cut_next,
        ),
        [pltpu.SMEM(offsets.shape, I32), pltpu.VMEM((per, side, LANES), F32), dma(())],
    )
    return density, gradient


def solution(mesh):
    return jax.shard_map(
        step,
        mesh=mesh,
        in_specs=(
            P("atoms", None, None, None),
            P("atoms", None),
            P(("atoms", "bricks"), None),
            P(("atoms", "bricks"), None),
            P("atoms", None, "bricks"),
        ),
        out_specs=(P("atoms", None, "bricks"), P(("atoms", "bricks"), None, None, None)),
        check_vma=False,
    )
```

```python
import jax
import jax.numpy as jnp
from jax import lax
from jax.experimental import pallas as pl
from jax.experimental.pallas import tpu as pltpu
from jax.sharding import PartitionSpec as P

LANES = 128
SUB = 8
F32 = jnp.float32
BF16 = jnp.bfloat16
I32 = jnp.int32
VMEM = pl.BlockSpec(memory_space=pltpu.VMEM)
HBM = pl.BlockSpec(memory_space=pltpu.HBM)
GRANT = 16 * 2**20


def iota(shape, dim):
    return lax.broadcasted_iota(I32, shape, dim)


def rows_splat(values, count):
    tiles = []
    for start in range(0, count, SUB):
        tile = jnp.zeros((SUB, LANES), F32)
        row = iota((SUB, LANES), 0)
        for r in range(SUB):
            if start + r < len(values) and values[start + r] is not None:
                tile = jnp.where(row == r, values[start + r], tile)
        tiles.append(tile)
    return jnp.concatenate(tiles, 0)


def pack_kernel(
    offs_hbm, kern_hbm, pat_hbm, orbs_hbm, v_hbm, out, v_out, offs, kern, pat, orb, sems
):
    core = lax.axis_index("bricks")
    copies = [
        pltpu.make_async_copy(src, dst, sems.at[n])
        for n, (src, dst) in enumerate(
            (
                (offs_hbm, offs),
                (kern_hbm, kern),
                (pat_hbm, pat),
                (orbs_hbm.at[core], orb),
                (v_hbm, v_out),
            )
        )
    ]
    for copy in copies:
        copy.start()
    count, side = orbs_hbm.shape[0], orb.shape[0]
    groups = LANES // side
    per = side // groups
    k_at, lane = iota((side, LANES), 0), iota((side, LANES), 1)
    for copy in copies[:-1]:
        copy.wait()
    corner = [offs[core, axis] for axis in range(3)]
    o0, o1, o2 = corner
    turned = (lane & (side - 1)) == ((k_at + o2) & (side - 1))
    total = jnp.zeros((per * side, LANES), F32)
    for g in range(groups):
        spread = jnp.where(turned & ((lane // side) == g), 1.0, 0.0).astype(BF16)
        planes = [orb[(g * per + i - o0) & (side - 1)] for i in range(per)]
        total = total + jnp.dot(jnp.concatenate(planes, 0), spread, preferred_element_type=F32)
    for i in range(per):
        plane = pltpu.roll(total[i * side : (i + 1) * side], o1 & (side - 1), 0)
        out[i] = plane.astype(BF16)
    values = [jnp.full((1, LANES), m, I32).astype(F32) for m in corner] + [None] * (SUB - 3)
    line = kern[...] * pat[...].astype(F32)
    spread = [jnp.broadcast_to(line[:, c : c + 1], (1, LANES)) for c in range(3 * count)]
    for c in range(3 * count):
        w = jnp.where(core == 0, spread[c], spread[c ^ 1])
        high = w.astype(BF16).astype(F32)
        values += [high, w - high]
    out[per] = rows_splat(values, side).astype(BF16)
    copies[-1].wait()


def cut_kernel(packet, offs_prev, v_own, v_other, cut_own, cut_prev):
    side, depth = v_own.shape[0], v_own.shape[1]
    groups = LANES // side
    per = side // groups
    core = lax.axis_index("bricks")
    meta = packet[packet.shape[0] - 1].astype(F32)
    line = jnp.where(core == 0, offs_prev[0:1, :], offs_prev[1:2, :])
    corners = [
        [meta[axis : axis + 1].astype(I32) for axis in range(3)],
        [jnp.broadcast_to(line[:, axis : axis + 1], (1, LANES)) for axis in range(3)],
    ]
    lane = iota((side, LANES), 1)
    row = iota((side, LANES), 0)
    fold = jnp.where((lane & (side - 1)) == row, 1.0, 0.0).astype(BF16)
    folds = []
    for g in range(groups):
        block = fold * jnp.where((lane // side) == g, 1.0, 0.0).astype(BF16)
        folds += [block] * groups
    folds = jnp.concatenate(folds, 0)
    for (_, o1, o2), cut in zip(corners, (cut_own, cut_prev)):
        upper = row < o1
        mine = ((lane - o2) & (LANES - 1)) < side
        start = o2 + ((lane - o2) & (LANES - 1))
        own = mine & ((start // LANES) == core)
        other = mine & ((start // LANES) != core)
        masks = [
            jnp.where(a & b, 1.0, 0.0).astype(BF16)
            for a in (own, other)
            for b in (~upper, upper)
        ]
        parts = []
        for g in range(groups):
            planes = []
            for x in range(g * per, (g + 1) * per):
                plane = None
                for n, (v, at) in enumerate(
                    ((v_own, 0), (v_own, depth - side), (v_other, 0), (v_other, depth - side))
                ):
                    term = v[x, at : at + side].astype(BF16) * masks[n]
                    plane = term if plane is None else plane + term
                planes.append(plane)
            parts.append(jnp.concatenate(planes, 0))
        out = jnp.dot(jnp.concatenate(parts, 1), folds, preferred_element_type=F32)
        cut[...] = out.astype(BF16).reshape(per, side, LANES)


class Tables:
    def __init__(self, packets, places):
        self.places = places
        self.metas = [packet[packet.shape[0] - 1].astype(F32) for packet in packets]
        self.corner = [
            [meta[axis : axis + 1].astype(I32) for axis in range(3)] for meta in self.metas
        ]

    def weight(self, a, b):
        (da, oa), (db, ob) = self.places[a], self.places[b]
        at = SUB + 2 * ((db - da + 1) * 2 + (oa ^ ob))
        return self.metas[a][at : at + 1] + self.metas[a][at + 1 : at + 2]

    def pair(self, a, b):
        return self.weight(a, b) if a == b else self.weight(a, b) + self.weight(b, a)


def brick_kernel(prev0, prev1, own0, own1, dens, ready, placed):
    core = lax.axis_index("bricks")
    side = dens.shape[0]
    groups = LANES // side
    per = side // groups
    packets = (prev0, prev1, own0, own1)
    many = len(packets)
    tables = Tables(packets, ((0, 0), (0, 1), (1, 0), (1, 1)))
    lane = iota((1, LANES), 1)
    k_at = lane & (side - 1)
    row = iota((side, LANES), 0)
    uppers = [row < tables.corner[b][1] for b in range(many)]
    z_at = [o2 + ((k_at - o2) & (side - 1)) for _, _, o2 in tables.corner]
    links = {}
    for a in range(many):
        for b in range(a, many):
            w = tables.pair(a, b)
            if a != b:
                w = jnp.where(uppers[a] == uppers[b], jnp.where(z_at[a] == z_at[b], w, 0.0), 0.0)
            links[a, b] = jnp.broadcast_to(w, (side, LANES))
    for i in range(per):
        x = (lane // side) * per + i
        fields = []
        for b in range(many):
            o0 = tables.corner[b][0]
            keep = (x < o0) if b < 2 else (x >= o0)
            kept = packets[b][i] * jnp.where(keep, 1.0, 0.0).astype(BF16)
            fields.append(kept.astype(F32))
        for a in range(many):
            inner = links[a, a] * fields[a]
            for b in range(a + 1, many):
                inner = inner + links[a, b] * fields[b]
            product = fields[a] * inner
            high = product.astype(BF16)
            ready[a, i * side : (i + 1) * side, 0:LANES] = high
            ready[a, i * side : (i + 1) * side, LANES:] = (product - high.astype(F32)).astype(BF16)
    wide = groups * LANES
    to = iota((LANES, wide), 1)
    from_lane = iota((LANES, wide), 0)
    spread = jnp.where(from_lane == (to // LANES) * side + (to & (side - 1)), 1.0, 0.0).astype(BF16)
    for a in range(many):
        inside = jnp.where(z_at[a] == core * LANES + lane, 1.0, 0.0).astype(BF16)
        place = spread * jnp.concatenate([inside] * groups, 1)
        out = jnp.dot(ready[a], jnp.concatenate([place] * 2, 0), preferred_element_type=F32)
        placed[a] = out
    for g in range(groups):
        for i in range(per):
            x = g * per + i
            parts = [placed[a, i * side : (i + 1) * side, g * LANES : (g + 1) * LANES] for a in range(many)]
            low, high = None, None
            for a in range(many):
                down = jnp.where(uppers[a], 0.0, parts[a])
                up = jnp.where(uppers[a], parts[a], 0.0)
                low = down if low is None else low + down
                high = up if high is None else high + up
            dens[x, 0:side] = low
            dens[x, side : 2 * side] = high


def box_kernel(
    offs_hbm,
    prev0,
    prev1,
    own0,
    own1,
    next0,
    next1,
    cut_own,
    cut_next,
    dens,
    dens_hbm,
    out,
    offs,
    grads,
    sems,
):
    copy = pltpu.make_async_copy(offs_hbm, offs, sems.at[0])
    copy.start()
    whole = pltpu.make_async_copy(dens, dens_hbm, sems.at[1])
    whole.start()
    core = lax.axis_index("bricks")
    side = out.shape[1]
    groups = LANES // side
    per = side // groups
    packets = (prev0, prev1, own0, own1, next0, next1)
    tables = Tables(packets, ((0, 0), (0, 1), (1, 0), (1, 1), (2, 0), (2, 1)))
    me, mate = 2, 3
    lane = iota((1, LANES), 1)
    k_at = lane & (side - 1)
    row = iota((side, LANES), 0)
    a0, a1, a2 = tables.corner[me]
    z_me = a2 + ((k_at - a2) & (side - 1))
    upper = row < a1

    def same_yz(b):
        _, o1, o2 = tables.corner[b]
        z = jnp.where(o2 + ((k_at - o2) & (side - 1)) == z_me, 1.0, 0.0)
        return jnp.where((row < o1) == upper, z, 0.0)

    overlap = [None if b == me else same_yz(b) for b in range(6)]
    inner_ids, last_ids = (0, 1, me, mate), (4, 5, me, mate)
    pair = {}
    for a in range(4):
        for b in range(a, 4):
            pair[a, b] = (
                tables.pair(inner_ids[a], inner_ids[b]), tables.pair(last_ids[a], last_ids[b])
            )
    mine = [(tables.weight(me, inner_ids[b]), tables.weight(me, last_ids[b])) for b in range(4)]
    for i in range(per):
        x = (lane // side) * per + i
        spill = x < a0

        def pick(both, a, b):
            return both[0] if a >= 2 and b >= 2 else jnp.where(spill, both[1], both[0])

        fields = []
        for o in (0, 1):
            before = jnp.where((x < tables.corner[o][0]) & ~spill, 1.0, 0.0).astype(BF16)
            after = jnp.where((x >= tables.corner[4 + o][0]) & spill, 1.0, 0.0).astype(BF16)
            fields.append(
                (packets[o][i] * before).astype(F32) * overlap[o]
                + (packets[4 + o][i] * after).astype(F32) * overlap[4 + o]
            )
        fields.append(packets[me][i].astype(F32))
        also = jnp.where((x < tables.corner[mate][0]) == spill, 1.0, 0.0).astype(BF16)
        fields.append((packets[mate][i] * also).astype(F32) * overlap[mate])
        rho = None
        for a in range(4):
            inner = None
            for b in range(a, 4):
                term = pick(pair[a, b], a, b) * fields[b]
                inner = term if inner is None else inner + term
            rho = fields[a] * inner if rho is None else rho + fields[a] * inner
        mix = None
        for b in range(4):
            term = pick(mine[b], b, me) * fields[b]
            mix = term if mix is None else mix + term
        bend = rho * lax.rsqrt(1.0 + rho * rho)
        outer = jnp.where(spill, cut_next[i].astype(F32), cut_own[i].astype(F32))
        potential = (outer + bend).astype(BF16).astype(F32)
        grads[i] = 2.0 * potential * mix
    copy.wait()
    s0, s1, s2 = offs[core, 0], offs[core, 1], offs[core, 2]
    planes = [pltpu.roll(grads[i], (side - s1) & (side - 1), 0).astype(BF16) for i in range(per)]
    stacked = jnp.concatenate(planes, 0)
    from_lane, to = iota((LANES, side), 0), iota((LANES, side), 1)
    turned = (from_lane & (side - 1)) == ((to + s2) & (side - 1))
    for g in range(groups):
        gather = jnp.where(turned & ((from_lane // side) == g), 1.0, 0.0).astype(BF16)
        part = jnp.dot(stacked, gather, preferred_element_type=F32).astype(BF16)
        for i in range(per):
            out[0, (g * per + i - s0) & (side - 1)] = part[i * side : (i + 1) * side]
    whole.wait()


def call(kernel, outs, out_specs, ins, args, scratch, moved=2000000):
    return pl.pallas_call(
        kernel,
        out_shape=outs,
        in_specs=ins,
        out_specs=out_specs,
        scratch_shapes=scratch,
        compiler_params=pltpu.CompilerParams(vmem_limit_bytes=GRANT),
        cost_estimate=pl.CostEstimate(
            flops=1000000, bytes_accessed=moved, transcendentals=0
        ),
    )(*[
        pltpu.with_memory_space_constraint(x, pltpu.HBM) if spec is HBM else x
        for x, spec in zip(args, ins)
    ])


def step(orbitals, offsets, kernel, pattern, local_potential):
    devices = lax.axis_size("atoms")
    up = [(i, (i + 1) % devices) for i in range(devices)]
    down = [(j, i) for i, j in up]
    swap = [(0, 1), (1, 0)]
    count, side = orbitals.shape[0], orbitals.shape[1]
    depth, width = local_potential.shape[1], local_potential.shape[2]
    groups = LANES // side
    per = side // groups
    shape = jax.ShapeDtypeStruct
    dma = pltpu.SemaphoreType.DMA
    offsets_prev = lax.ppermute(offsets, "atoms", up)
    own, mine = call(
        pack_kernel,
        (shape((per + 1, side, LANES), BF16), shape(local_potential.shape, F32)),
        (VMEM,) * 2,
        [HBM] * 5,
        (offsets, kernel, pattern, orbitals, local_potential),
        [
            pltpu.SMEM(offsets.shape, I32),
            pltpu.VMEM(kernel.shape, F32),
            pltpu.VMEM(pattern.shape, I32),
            pltpu.VMEM(orbitals.shape[1:], BF16),
            dma((5,)),
        ],
    )
    prev = lax.ppermute(own, "atoms", up)
    following = lax.ppermute(own, "atoms", down)
    other = lax.ppermute(local_potential, "bricks", swap)
    own_mate = lax.ppermute(own, "bricks", swap)
    cut_own, cut_prev = call(
        cut_kernel,
        (shape((per, side, LANES), BF16),) * 2,
        (VMEM,) * 2,
        [VMEM] * 4,
        (own, offsets_prev, mine, other),
        [],
    )
    cut_next = lax.ppermute(cut_prev, "atoms", down)
    prev_mate = lax.ppermute(prev, "bricks", swap)
    following_mate = lax.ppermute(following, "bricks", swap)
    dens = call(
        brick_kernel,
        shape((side, depth, width), F32),
        VMEM,
        [VMEM] * 4,
        (prev, prev_mate, own, own_mate),
        [
            pltpu.VMEM((2 * count, per * side, 2 * LANES), BF16),
            pltpu.VMEM((2 * count, per * side, groups * LANES), F32),
        ],
    )
    density, gradient = call(
        box_kernel,
        (shape((side, depth, width), F32), shape((1, side, side, side), BF16)),
        (HBM, VMEM),
        [HBM] + [VMEM] * 9,
        (
            offsets,
            prev,
            prev_mate,
            own,
            own_mate,
            following,
            following_mate,
            cut_own,
            cut_next,
            dens,
        ),
        [pltpu.SMEM(offsets.shape, I32), pltpu.VMEM((per, side, LANES), F32), dma((2,))],
    )
    return density, gradient


def solution(mesh):
    return jax.shard_map(
        step,
        mesh=mesh,
        in_specs=(
            P("atoms", None, None, None),
            P("atoms", None),
            P(("atoms", "bricks"), None),
            P(("atoms", "bricks"), None),
            P("atoms", None, "bricks"),
        ),
        out_specs=(P("atoms", None, "bricks"), P(("atoms", "bricks"), None, None, None)),
        check_vma=False,
    )
```

```python
import jax
import jax.numpy as jnp
from jax import lax
from jax.experimental import pallas as pl
from jax.experimental.pallas import tpu as pltpu
from jax.sharding import PartitionSpec as P

LANES = 128
SUB = 8
F32 = jnp.float32
BF16 = jnp.bfloat16
I32 = jnp.int32
VMEM = pl.BlockSpec(memory_space=pltpu.VMEM)
HBM = pl.BlockSpec(memory_space=pltpu.HBM)
GRANT = 16 * 2**20


def iota(shape, dim):
    return lax.broadcasted_iota(I32, shape, dim)


def rows_splat(values, count):
    tiles = []
    for start in range(0, count, SUB):
        tile = jnp.zeros((SUB, LANES), F32)
        row = iota((SUB, LANES), 0)
        for r in range(SUB):
            if start + r < len(values) and values[start + r] is not None:
                tile = jnp.where(row == r, values[start + r], tile)
        tiles.append(tile)
    return jnp.concatenate(tiles, 0)


def pack_kernel(
    offs_hbm, kern_hbm, pat_hbm, orbs_hbm, v_hbm, out, v_out, offs, kern, pat, orb, sems
):
    core = lax.axis_index("bricks")
    copies = [
        pltpu.make_async_copy(src, dst, sems.at[n])
        for n, (src, dst) in enumerate(
            (
                (offs_hbm, offs),
                (kern_hbm, kern),
                (pat_hbm, pat),
                (orbs_hbm.at[core], orb),
                (v_hbm, v_out),
            )
        )
    ]
    for copy in copies:
        copy.start()
    count, side = orbs_hbm.shape[0], orb.shape[0]
    groups = LANES // side
    per = side // groups
    k_at, lane = iota((side, LANES), 0), iota((side, LANES), 1)
    for copy in copies[:-1]:
        copy.wait()
    corner = [offs[core, axis] for axis in range(3)]
    o0, o1, o2 = corner
    turned = (lane & (side - 1)) == ((k_at + o2) & (side - 1))
    total = jnp.zeros((per * side, LANES), F32)
    for g in range(groups):
        spread = jnp.where(turned & ((lane // side) == g), 1.0, 0.0).astype(BF16)
        planes = [orb[(g * per + i - o0) & (side - 1)] for i in range(per)]
        total = total + jnp.dot(jnp.concatenate(planes, 0), spread, preferred_element_type=F32)
    for i in range(per):
        plane = pltpu.roll(total[i * side : (i + 1) * side], o1 & (side - 1), 0)
        out[i] = plane.astype(BF16)
    values = [jnp.full((1, LANES), m, I32).astype(F32) for m in corner] + [None] * (SUB - 3)
    line = kern[...] * pat[...].astype(F32)
    spread = [jnp.broadcast_to(line[:, c : c + 1], (1, LANES)) for c in range(3 * count)]
    for c in range(3 * count):
        w = jnp.where(core == 0, spread[c], spread[c ^ 1])
        high = w.astype(BF16).astype(F32)
        values += [high, w - high]
    out[per] = rows_splat(values, side).astype(BF16)
    copies[-1].wait()


def cut_kernel(packet, offs_prev, v_own, v_other, cut_own, cut_prev):
    side, depth = v_own.shape[0], v_own.shape[1]
    groups = LANES // side
    per = side // groups
    core = lax.axis_index("bricks")
    meta = packet[packet.shape[0] - 1].astype(F32)
    line = jnp.where(core == 0, offs_prev[0:1, :], offs_prev[1:2, :])
    corners = [
        [meta[axis : axis + 1].astype(I32) for axis in range(3)],
        [jnp.broadcast_to(line[:, axis : axis + 1], (1, LANES)) for axis in range(3)],
    ]
    lane = iota((side, LANES), 1)
    row = iota((side, LANES), 0)
    fold = jnp.where((lane & (side - 1)) == row, 1.0, 0.0).astype(BF16)
    folds = []
    for g in range(groups):
        block = fold * jnp.where((lane // side) == g, 1.0, 0.0).astype(BF16)
        folds += [block] * groups
    folds = jnp.concatenate(folds, 0)
    for (_, o1, o2), cut in zip(corners, (cut_own, cut_prev)):
        upper = row < o1
        mine = ((lane - o2) & (LANES - 1)) < side
        start = o2 + ((lane - o2) & (LANES - 1))
        own = mine & ((start // LANES) == core)
        other = mine & ((start // LANES) != core)
        masks = [
            jnp.where(a & b, 1.0, 0.0).astype(BF16)
            for a in (own, other)
            for b in (~upper, upper)
        ]
        parts = []
        for g in range(groups):
            planes = []
            for x in range(g * per, (g + 1) * per):
                plane = None
                for n, (v, at) in enumerate(
                    ((v_own, 0), (v_own, depth - side), (v_other, 0), (v_other, depth - side))
                ):
                    term = v[x, at : at + side].astype(BF16) * masks[n]
                    plane = term if plane is None else plane + term
                planes.append(plane)
            parts.append(jnp.concatenate(planes, 0))
        out = jnp.dot(jnp.concatenate(parts, 1), folds, preferred_element_type=F32)
        cut[...] = out.astype(BF16).reshape(per, side, LANES)


class Tables:
    def __init__(self, packets, places):
        self.places = places
        self.metas = [packet[packet.shape[0] - 1].astype(F32) for packet in packets]
        self.corner = [
            [meta[axis : axis + 1].astype(I32) for axis in range(3)] for meta in self.metas
        ]

    def weight(self, a, b):
        (da, oa), (db, ob) = self.places[a], self.places[b]
        at = SUB + 2 * ((db - da + 1) * 2 + (oa ^ ob))
        return self.metas[a][at : at + 1] + self.metas[a][at + 1 : at + 2]

    def pair(self, a, b):
        return self.weight(a, b) if a == b else self.weight(a, b) + self.weight(b, a)


def fill_brick(prev0, prev1, own0, own1, dens, ready, placed):
    core = lax.axis_index("bricks")
    side = dens.shape[0]
    groups = LANES // side
    per = side // groups
    packets = (prev0, prev1, own0, own1)
    many = len(packets)
    tables = Tables(packets, ((0, 0), (0, 1), (1, 0), (1, 1)))
    lane = iota((1, LANES), 1)
    k_at = lane & (side - 1)
    row = iota((side, LANES), 0)
    uppers = [row < tables.corner[b][1] for b in range(many)]
    z_at = [o2 + ((k_at - o2) & (side - 1)) for _, _, o2 in tables.corner]
    links = {}
    for a in range(many):
        for b in range(a, many):
            w = tables.pair(a, b)
            if a != b:
                w = jnp.where(uppers[a] == uppers[b], jnp.where(z_at[a] == z_at[b], w, 0.0), 0.0)
            links[a, b] = jnp.broadcast_to(w, (side, LANES))
    for i in range(per):
        x = (lane // side) * per + i
        fields = []
        for b in range(many):
            o0 = tables.corner[b][0]
            keep = (x < o0) if b < 2 else (x >= o0)
            kept = packets[b][i] * jnp.where(keep, 1.0, 0.0).astype(BF16)
            fields.append(kept.astype(F32))
        for a in range(many):
            inner = links[a, a] * fields[a]
            for b in range(a + 1, many):
                inner = inner + links[a, b] * fields[b]
            product = fields[a] * inner
            high = product.astype(BF16)
            ready[a, i * side : (i + 1) * side, 0:LANES] = high
            ready[a, i * side : (i + 1) * side, LANES:] = (product - high.astype(F32)).astype(BF16)
    wide = groups * LANES
    to = iota((LANES, wide), 1)
    from_lane = iota((LANES, wide), 0)
    spread = jnp.where(from_lane == (to // LANES) * side + (to & (side - 1)), 1.0, 0.0).astype(BF16)
    for a in range(many):
        inside = jnp.where(z_at[a] == core * LANES + lane, 1.0, 0.0).astype(BF16)
        place = spread * jnp.concatenate([inside] * groups, 1)
        out = jnp.dot(ready[a], jnp.concatenate([place] * 2, 0), preferred_element_type=F32)
        placed[a] = out
    for g in range(groups):
        for i in range(per):
            x = g * per + i
            parts = [placed[a, i * side : (i + 1) * side, g * LANES : (g + 1) * LANES] for a in range(many)]
            low, high = None, None
            for a in range(many):
                down = jnp.where(uppers[a], 0.0, parts[a])
                up = jnp.where(uppers[a], parts[a], 0.0)
                low = down if low is None else low + down
                high = up if high is None else high + up
            dens[x, 0:side] = low
            dens[x, side : 2 * side] = high


def mid_kernel(
    prev0, prev1, own0, own1, next0, next1, dens, mixed, bend, ready, placed
):
    side, per = own0.shape[1], own0.shape[0] - 1
    fill_brick(prev0, prev1, own0, own1, dens, ready, placed)
    packets = (prev0, prev1, own0, own1, next0, next1)
    tables = Tables(packets, ((0, 0), (0, 1), (1, 0), (1, 1), (2, 0), (2, 1)))
    me, mate = 2, 3
    lane = iota((1, LANES), 1)
    k_at = lane & (side - 1)
    row = iota((side, LANES), 0)
    a0, a1, a2 = tables.corner[me]
    z_me = a2 + ((k_at - a2) & (side - 1))
    upper = row < a1

    def same_yz(b):
        _, o1, o2 = tables.corner[b]
        z = jnp.where(o2 + ((k_at - o2) & (side - 1)) == z_me, 1.0, 0.0)
        return jnp.where((row < o1) == upper, z, 0.0)

    overlap = [None if b == me else same_yz(b) for b in range(6)]
    inner_ids, last_ids = (0, 1, me, mate), (4, 5, me, mate)
    pair = {}
    for a in range(4):
        for b in range(a, 4):
            pair[a, b] = (
                tables.pair(inner_ids[a], inner_ids[b]), tables.pair(last_ids[a], last_ids[b])
            )
    mine = [(tables.weight(me, inner_ids[b]), tables.weight(me, last_ids[b])) for b in range(4)]
    for i in range(per):
        x = (lane // side) * per + i
        spill = x < a0

        def pick(both, a, b):
            return both[0] if a >= 2 and b >= 2 else jnp.where(spill, both[1], both[0])

        fields = []
        for o in (0, 1):
            before = jnp.where((x < tables.corner[o][0]) & ~spill, 1.0, 0.0).astype(BF16)
            after = jnp.where((x >= tables.corner[4 + o][0]) & spill, 1.0, 0.0).astype(BF16)
            fields.append(
                (packets[o][i] * before).astype(F32) * overlap[o]
                + (packets[4 + o][i] * after).astype(F32) * overlap[4 + o]
            )
        fields.append(packets[me][i].astype(F32))
        also = jnp.where((x < tables.corner[mate][0]) == spill, 1.0, 0.0).astype(BF16)
        fields.append((packets[mate][i] * also).astype(F32) * overlap[mate])
        rho = None
        for a in range(4):
            inner = None
            for b in range(a, 4):
                term = pick(pair[a, b], a, b) * fields[b]
                inner = term if inner is None else inner + term
            rho = fields[a] * inner if rho is None else rho + fields[a] * inner
        mix = None
        for b in range(4):
            term = pick(mine[b], b, me) * fields[b]
            mix = term if mix is None else mix + term
        mixed[i] = mix
        bend[i] = rho * lax.rsqrt(1.0 + rho * rho)


def last_kernel(own, cut_own, cut_next, mixed, bend, dens, dens_hbm, out_hbm, out, sems):
    copies = [
        pltpu.make_async_copy(dens, dens_hbm, sems.at[0]),
        pltpu.make_async_copy(out, out_hbm, sems.at[1]),
    ]
    copies[0].start()
    side = out.shape[1]
    groups = LANES // side
    per = side // groups
    corner = own[per, 0:SUB].astype(F32).astype(I32)
    s0, s1, s2 = [corner[axis, 0] for axis in range(3)]
    lane = iota((1, LANES), 1)
    planes = []
    for i in range(per):
        spill = (lane // side) * per + i < s0
        outer = jnp.where(spill, cut_next[i].astype(F32), cut_own[i].astype(F32))
        potential = (outer + bend[i]).astype(BF16).astype(F32)
        grad = 2.0 * potential * mixed[i]
        planes.append(pltpu.roll(grad, (side - s1) & (side - 1), 0).astype(BF16))
    stacked = jnp.concatenate(planes, 0)
    from_lane, to = iota((LANES, side), 0), iota((LANES, side), 1)
    turned = (from_lane & (side - 1)) == ((to + s2) & (side - 1))
    for g in range(groups):
        gather = jnp.where(turned & ((from_lane // side) == g), 1.0, 0.0).astype(BF16)
        part = jnp.dot(stacked, gather, preferred_element_type=F32).astype(BF16)
        for i in range(per):
            out[0, (g * per + i - s0) & (side - 1)] = part[i * side : (i + 1) * side]
    copies[1].start()
    for copy in copies:
        copy.wait()


def call(kernel, outs, out_specs, ins, args, scratch, moved=2000000):
    return pl.pallas_call(
        kernel,
        out_shape=outs,
        in_specs=ins,
        out_specs=out_specs,
        scratch_shapes=scratch,
        compiler_params=pltpu.CompilerParams(vmem_limit_bytes=GRANT),
        cost_estimate=pl.CostEstimate(
            flops=1000000, bytes_accessed=moved, transcendentals=0
        ),
    )(*[
        pltpu.with_memory_space_constraint(x, pltpu.HBM) if spec is HBM else x
        for x, spec in zip(args, ins)
    ])


def step(orbitals, offsets, kernel, pattern, local_potential):
    devices = lax.axis_size("atoms")
    up = [(i, (i + 1) % devices) for i in range(devices)]
    down = [(j, i) for i, j in up]
    swap = [(0, 1), (1, 0)]
    count, side = orbitals.shape[0], orbitals.shape[1]
    depth, width = local_potential.shape[1], local_potential.shape[2]
    groups = LANES // side
    per = side // groups
    shape = jax.ShapeDtypeStruct
    dma = pltpu.SemaphoreType.DMA
    offsets_prev = lax.ppermute(offsets, "atoms", up)
    own, mine = call(
        pack_kernel,
        (shape((per + 1, side, LANES), BF16), shape(local_potential.shape, F32)),
        (VMEM,) * 2,
        [HBM] * 5,
        (offsets, kernel, pattern, orbitals, local_potential),
        [
            pltpu.SMEM(offsets.shape, I32),
            pltpu.VMEM(kernel.shape, F32),
            pltpu.VMEM(pattern.shape, I32),
            pltpu.VMEM(orbitals.shape[1:], BF16),
            dma((5,)),
        ],
    )
    prev = lax.ppermute(own, "atoms", up)
    following = lax.ppermute(own, "atoms", down)
    other = lax.ppermute(local_potential, "bricks", swap)
    own_mate = lax.ppermute(own, "bricks", swap)
    cut_own, cut_prev = call(
        cut_kernel,
        (shape((per, side, LANES), BF16),) * 2,
        (VMEM,) * 2,
        [VMEM] * 4,
        (own, offsets_prev, mine, other),
        [],
    )
    cut_next = lax.ppermute(cut_prev, "atoms", down)
    prev_mate = lax.ppermute(prev, "bricks", swap)
    following_mate = lax.ppermute(following, "bricks", swap)
    dens, mixed, bend = call(
        mid_kernel,
        (shape((side, depth, width), F32),) + (shape((per, side, LANES), F32),) * 2,
        (VMEM,) * 3,
        [VMEM] * 6,
        (prev, prev_mate, own, own_mate, following, following_mate),
        [
            pltpu.VMEM((2 * count, per * side, 2 * LANES), BF16),
            pltpu.VMEM((2 * count, per * side, groups * LANES), F32),
        ],
    )
    density, gradient = call(
        last_kernel,
        (shape((side, depth, width), F32), shape((1, side, side, side), BF16)),
        (HBM,) * 2,
        [VMEM] * 6,
        (own, cut_own, cut_next, mixed, bend, dens),
        [pltpu.VMEM((1, side, side, side), BF16), dma((2,))],
    )
    return density, gradient


def solution(mesh):
    return jax.shard_map(
        step,
        mesh=mesh,
        in_specs=(
            P("atoms", None, None, None),
            P("atoms", None),
            P(("atoms", "bricks"), None),
            P(("atoms", "bricks"), None),
            P("atoms", None, "bricks"),
        ),
        out_specs=(P("atoms", None, "bricks"), P(("atoms", "bricks"), None, None, None)),
        check_vma=False,
    )
```

```python
import jax
import jax.numpy as jnp
from jax import lax
from jax.experimental import pallas as pl
from jax.experimental.pallas import tpu as pltpu
from jax.sharding import PartitionSpec as P

LANES = 128
SUB = 8
F32 = jnp.float32
BF16 = jnp.bfloat16
I32 = jnp.int32
VMEM = pl.BlockSpec(memory_space=pltpu.VMEM)
HBM = pl.BlockSpec(memory_space=pltpu.HBM)
GRANT = 16 * 2**20


def iota(shape, dim):
    return lax.broadcasted_iota(I32, shape, dim)


def rows_splat(values, count):
    tiles = []
    for start in range(0, count, SUB):
        tile = jnp.zeros((SUB, LANES), F32)
        row = iota((SUB, LANES), 0)
        for r in range(SUB):
            if start + r < len(values) and values[start + r] is not None:
                tile = jnp.where(row == r, values[start + r], tile)
        tiles.append(tile)
    return jnp.concatenate(tiles, 0)


def pack_kernel(
    offs_hbm, kern_hbm, pat_hbm, orbs_hbm, v_hbm, out, v_out, offs, kern, pat, orb, sems
):
    core = lax.axis_index("bricks")
    copies = [
        pltpu.make_async_copy(src, dst, sems.at[n])
        for n, (src, dst) in enumerate(
            (
                (offs_hbm, offs),
                (kern_hbm, kern),
                (pat_hbm, pat),
                (orbs_hbm.at[core], orb),
                (v_hbm, v_out),
            )
        )
    ]
    for copy in copies:
        copy.start()
    count, side = orbs_hbm.shape[0], orb.shape[0]
    groups = LANES // side
    per = side // groups
    k_at, lane = iota((side, LANES), 0), iota((side, LANES), 1)
    for copy in copies[:3]:
        copy.wait()
    table = offs[...]
    corner = [jnp.where(core == 0, table[0, axis], table[1, axis]) for axis in range(3)]
    o0, o1, o2 = corner
    turned = jnp.where((lane & (side - 1)) == ((k_at + o2) & (side - 1)), 1.0, 0.0)
    spreads = [jnp.where((lane // side) == g, turned, 0.0).astype(BF16) for g in range(groups)]
    values = [jnp.full((1, LANES), m, I32).astype(F32) for m in corner] + [None] * (SUB - 3)
    line = kern[...] * pat[...].astype(F32)
    wide = [jnp.broadcast_to(line[:, c : c + 1], (1, LANES)) for c in range(3 * count)]
    for c in range(3 * count):
        w = jnp.where(core == 0, wide[c], wide[c ^ 1])
        high = w.astype(BF16).astype(F32)
        values += [high, w - high]
    out[per] = rows_splat(values, side).astype(BF16)
    copies[3].wait()
    total = jnp.zeros((per * side, LANES), F32)
    for g in range(groups):
        planes = [orb[(g * per + i - o0) & (side - 1)] for i in range(per)]
        total = total + jnp.dot(
            jnp.concatenate(planes, 0), spreads[g], preferred_element_type=F32
        )
    for i in range(per):
        plane = pltpu.roll(total[i * side : (i + 1) * side], o1 & (side - 1), 0)
        out[i] = plane.astype(BF16)
    copies[4].wait()


def cut_kernel(packet, offs_prev, v_own, v_other, cut_own, cut_prev):
    side, depth = v_own.shape[0], v_own.shape[1]
    groups = LANES // side
    per = side // groups
    core = lax.axis_index("bricks")
    meta = packet[packet.shape[0] - 1].astype(F32)
    line = jnp.where(core == 0, offs_prev[0:1, :], offs_prev[1:2, :])
    corners = [
        [meta[axis : axis + 1].astype(I32) for axis in range(3)],
        [jnp.broadcast_to(line[:, axis : axis + 1], (1, LANES)) for axis in range(3)],
    ]
    lane = iota((side, LANES), 1)
    row = iota((side, LANES), 0)
    fold = jnp.where((lane & (side - 1)) == row, 1.0, 0.0).astype(BF16)
    folds = []
    for g in range(groups):
        block = fold * jnp.where((lane // side) == g, 1.0, 0.0).astype(BF16)
        folds += [block] * groups
    folds = jnp.concatenate(folds, 0)
    for (_, o1, o2), cut in zip(corners, (cut_own, cut_prev)):
        upper = row < o1
        mine = ((lane - o2) & (LANES - 1)) < side
        start = o2 + ((lane - o2) & (LANES - 1))
        own = mine & ((start // LANES) == core)
        other = mine & ((start // LANES) != core)
        high, left, right = [
            jnp.where(m, 1.0, 0.0).astype(BF16) > 0 for m in (upper, own, other)
        ]
        zero = jnp.zeros((side, LANES), BF16)
        parts = []
        for g in range(groups):
            planes = []
            for x in range(g * per, (g + 1) * per):
                one, two = [
                    jnp.where(
                        high, v[x, depth - side :].astype(BF16), v[x, 0:side].astype(BF16)
                    )
                    for v in (v_own, v_other)
                ]
                plane = jnp.where(left, one, jnp.where(right, two, zero))
                planes.append(plane)
            parts.append(jnp.concatenate(planes, 0))
        out = jnp.dot(jnp.concatenate(parts, 1), folds, preferred_element_type=F32)
        cut[...] = out.astype(BF16).reshape(per, side, LANES)


class Tables:
    def __init__(self, packets, places):
        self.places = places
        self.metas = [packet[packet.shape[0] - 1].astype(F32) for packet in packets]
        self.corner = [
            [meta[axis : axis + 1].astype(I32) for axis in range(3)] for meta in self.metas
        ]

    def weight(self, a, b):
        (da, oa), (db, ob) = self.places[a], self.places[b]
        at = SUB + 2 * ((db - da + 1) * 2 + (oa ^ ob))
        return self.metas[a][at : at + 1] + self.metas[a][at + 1 : at + 2]

    def pair(self, a, b):
        return self.weight(a, b) if a == b else self.weight(a, b) + self.weight(b, a)


def fill_brick(prev0, prev1, own0, own1, dens, ready, placed):
    core = lax.axis_index("bricks")
    side = dens.shape[0]
    groups = LANES // side
    per = side // groups
    packets = (prev0, prev1, own0, own1)
    many = len(packets)
    tables = Tables(packets, ((0, 0), (0, 1), (1, 0), (1, 1)))
    lane = iota((1, LANES), 1)
    k_at = lane & (side - 1)
    row = iota((side, LANES), 0)
    uppers = [row < tables.corner[b][1] for b in range(many)]
    z_at = [o2 + ((k_at - o2) & (side - 1)) for _, _, o2 in tables.corner]
    links = {}
    for a in range(many):
        for b in range(a, many):
            w = tables.pair(a, b)
            if a != b:
                w = jnp.where(uppers[a] == uppers[b], jnp.where(z_at[a] == z_at[b], w, 0.0), 0.0)
            links[a, b] = jnp.broadcast_to(w, (side, LANES))
    for i in range(per):
        x = (lane // side) * per + i
        fields = []
        for b in range(many):
            o0 = tables.corner[b][0]
            keep = (x < o0) if b < 2 else (x >= o0)
            kept = packets[b][i] * jnp.where(keep, 1.0, 0.0).astype(BF16)
            fields.append(kept.astype(F32))
        for a in range(many):
            inner = links[a, a] * fields[a]
            for b in range(a + 1, many):
                inner = inner + links[a, b] * fields[b]
            product = fields[a] * inner
            high = product.astype(BF16)
            ready[a, i * side : (i + 1) * side, 0:LANES] = high
            ready[a, i * side : (i + 1) * side, LANES:] = (product - high.astype(F32)).astype(BF16)
    wide = groups * LANES
    to = iota((LANES, wide), 1)
    from_lane = iota((LANES, wide), 0)
    spread = jnp.where(from_lane == (to // LANES) * side + (to & (side - 1)), 1.0, 0.0).astype(BF16)
    for a in range(many):
        inside = jnp.where(z_at[a] == core * LANES + lane, 1.0, 0.0).astype(BF16)
        place = spread * jnp.concatenate([inside] * groups, 1)
        out = jnp.dot(ready[a], jnp.concatenate([place] * 2, 0), preferred_element_type=F32)
        placed[a] = out
    for g in range(groups):
        for i in range(per):
            x = g * per + i
            parts = [placed[a, i * side : (i + 1) * side, g * LANES : (g + 1) * LANES] for a in range(many)]
            low, high = None, None
            for a in range(many):
                down = jnp.where(uppers[a], 0.0, parts[a])
                up = jnp.where(uppers[a], parts[a], 0.0)
                low = down if low is None else low + down
                high = up if high is None else high + up
            dens[x, 0:side] = low
            dens[x, side : 2 * side] = high


def mid_kernel(
    prev0, prev1, own0, own1, next0, next1, dens, mixed, bend, ready, placed
):
    side, per = own0.shape[1], own0.shape[0] - 1
    fill_brick(prev0, prev1, own0, own1, dens, ready, placed)
    packets = (prev0, prev1, own0, own1, next0, next1)
    tables = Tables(packets, ((0, 0), (0, 1), (1, 0), (1, 1), (2, 0), (2, 1)))
    me, mate = 2, 3
    lane = iota((1, LANES), 1)
    k_at = lane & (side - 1)
    row = iota((side, LANES), 0)
    a0, a1, a2 = tables.corner[me]
    z_me = a2 + ((k_at - a2) & (side - 1))
    upper = row < a1

    def same_yz(b):
        _, o1, o2 = tables.corner[b]
        z = jnp.where(o2 + ((k_at - o2) & (side - 1)) == z_me, 1.0, 0.0)
        return jnp.where((row < o1) == upper, z, 0.0)

    overlap = [None if b == me else same_yz(b) for b in range(6)]
    inner_ids, last_ids = (0, 1, me, mate), (4, 5, me, mate)
    pair = {}
    for a in range(4):
        for b in range(a, 4):
            pair[a, b] = (
                tables.pair(inner_ids[a], inner_ids[b]), tables.pair(last_ids[a], last_ids[b])
            )
    mine = [(tables.weight(me, inner_ids[b]), tables.weight(me, last_ids[b])) for b in range(4)]
    for i in range(per):
        x = (lane // side) * per + i
        spill = x < a0

        def pick(both, a, b):
            return both[0] if a >= 2 and b >= 2 else jnp.where(spill, both[1], both[0])

        fields = []
        for o in (0, 1):
            before = jnp.where((x < tables.corner[o][0]) & ~spill, 1.0, 0.0).astype(BF16)
            after = jnp.where((x >= tables.corner[4 + o][0]) & spill, 1.0, 0.0).astype(BF16)
            fields.append(
                (packets[o][i] * before).astype(F32) * overlap[o]
                + (packets[4 + o][i] * after).astype(F32) * overlap[4 + o]
            )
        fields.append(packets[me][i].astype(F32))
        also = jnp.where((x < tables.corner[mate][0]) == spill, 1.0, 0.0).astype(BF16)
        fields.append((packets[mate][i] * also).astype(F32) * overlap[mate])
        rho = None
        for a in range(4):
            inner = None
            for b in range(a, 4):
                term = pick(pair[a, b], a, b) * fields[b]
                inner = term if inner is None else inner + term
            rho = fields[a] * inner if rho is None else rho + fields[a] * inner
        mix = None
        for b in range(4):
            term = pick(mine[b], b, me) * fields[b]
            mix = term if mix is None else mix + term
        mixed[i] = mix
        bend[i] = rho * lax.rsqrt(1.0 + rho * rho)


def last_kernel(own, cut_own, cut_next, mixed, bend, dens, dens_hbm, out_hbm, out, sems):
    copies = [
        pltpu.make_async_copy(dens, dens_hbm, sems.at[0]),
        pltpu.make_async_copy(out, out_hbm, sems.at[1]),
    ]
    copies[0].start()
    side = out.shape[1]
    groups = LANES // side
    per = side // groups
    corner = own[per, 0:SUB].astype(F32).astype(I32)
    s0, s1, s2 = [corner[axis, 0] for axis in range(3)]
    lane = iota((1, LANES), 1)
    planes = []
    for i in range(per):
        spill = (lane // side) * per + i < s0
        outer = jnp.where(spill, cut_next[i].astype(F32), cut_own[i].astype(F32))
        potential = (outer + bend[i]).astype(BF16).astype(F32)
        grad = 2.0 * potential * mixed[i]
        planes.append(pltpu.roll(grad, (side - s1) & (side - 1), 0).astype(BF16))
    stacked = jnp.concatenate(planes, 0)
    from_lane, to = iota((LANES, side), 0), iota((LANES, side), 1)
    turned = (from_lane & (side - 1)) == ((to + s2) & (side - 1))
    for g in range(groups):
        gather = jnp.where(turned & ((from_lane // side) == g), 1.0, 0.0).astype(BF16)
        part = jnp.dot(stacked, gather, preferred_element_type=F32).astype(BF16)
        for i in range(per):
            out[0, (g * per + i - s0) & (side - 1)] = part[i * side : (i + 1) * side]
    copies[1].start()
    for copy in copies:
        copy.wait()


def call(kernel, outs, out_specs, ins, args, scratch, moved=2000000):
    return pl.pallas_call(
        kernel,
        out_shape=outs,
        in_specs=ins,
        out_specs=out_specs,
        scratch_shapes=scratch,
        compiler_params=pltpu.CompilerParams(vmem_limit_bytes=GRANT),
        cost_estimate=pl.CostEstimate(
            flops=1000000, bytes_accessed=moved, transcendentals=0
        ),
    )(*[
        pltpu.with_memory_space_constraint(x, pltpu.HBM) if spec is HBM else x
        for x, spec in zip(args, ins)
    ])


def step(orbitals, offsets, kernel, pattern, local_potential):
    devices = lax.axis_size("atoms")
    up = [(i, (i + 1) % devices) for i in range(devices)]
    down = [(j, i) for i, j in up]
    swap = [(0, 1), (1, 0)]
    count, side = orbitals.shape[0], orbitals.shape[1]
    depth, width = local_potential.shape[1], local_potential.shape[2]
    groups = LANES // side
    per = side // groups
    shape = jax.ShapeDtypeStruct
    dma = pltpu.SemaphoreType.DMA
    offsets_prev = lax.ppermute(offsets, "atoms", up)
    own, mine = call(
        pack_kernel,
        (shape((per + 1, side, LANES), BF16), shape(local_potential.shape, F32)),
        (VMEM,) * 2,
        [HBM] * 5,
        (offsets, kernel, pattern, orbitals, local_potential),
        [
            pltpu.VMEM(offsets.shape, I32),
            pltpu.VMEM(kernel.shape, F32),
            pltpu.VMEM(pattern.shape, I32),
            pltpu.VMEM(orbitals.shape[1:], BF16),
            dma((5,)),
        ],
    )
    prev = lax.ppermute(own, "atoms", up)
    following = lax.ppermute(own, "atoms", down)
    other = lax.ppermute(local_potential, "bricks", swap)
    own_mate = lax.ppermute(own, "bricks", swap)
    cut_own, cut_prev = call(
        cut_kernel,
        (shape((per, side, LANES), BF16),) * 2,
        (VMEM,) * 2,
        [VMEM] * 4,
        (own, offsets_prev, mine, other),
        [],
    )
    cut_next = lax.ppermute(cut_prev, "atoms", down)
    prev_mate = lax.ppermute(prev, "bricks", swap)
    following_mate = lax.ppermute(following, "bricks", swap)
    dens, mixed, bend = call(
        mid_kernel,
        (shape((side, depth, width), F32),) + (shape((per, side, LANES), F32),) * 2,
        (VMEM,) * 3,
        [VMEM] * 6,
        (prev, prev_mate, own, own_mate, following, following_mate),
        [
            pltpu.VMEM((2 * count, per * side, 2 * LANES), BF16),
            pltpu.VMEM((2 * count, per * side, groups * LANES), F32),
        ],
    )
    density, gradient = call(
        last_kernel,
        (shape((side, depth, width), F32), shape((1, side, side, side), BF16)),
        (HBM,) * 2,
        [VMEM] * 6,
        (own, cut_own, cut_next, mixed, bend, dens),
        [pltpu.VMEM((1, side, side, side), BF16), dma((2,))],
    )
    return density, gradient


def solution(mesh):
    return jax.shard_map(
        step,
        mesh=mesh,
        in_specs=(
            P("atoms", None, None, None),
            P("atoms", None),
            P(("atoms", "bricks"), None),
            P(("atoms", "bricks"), None),
            P("atoms", None, "bricks"),
        ),
        out_specs=(P("atoms", None, "bricks"), P(("atoms", "bricks"), None, None, None)),
        check_vma=False,
    )
```

```python
import jax
import jax.numpy as jnp
from jax import lax
from jax.experimental import pallas as pl
from jax.experimental.pallas import tpu as pltpu
from jax.sharding import PartitionSpec as P

LANES = 128
SUB = 8
F32 = jnp.float32
BF16 = jnp.bfloat16
I32 = jnp.int32
VMEM = pl.BlockSpec(memory_space=pltpu.VMEM)
HBM = pl.BlockSpec(memory_space=pltpu.HBM)
GRANT = 16 * 2**20


def iota(shape, dim):
    return lax.broadcasted_iota(I32, shape, dim)


def rows_splat(values, count):
    tiles = []
    for start in range(0, count, SUB):
        tile = jnp.zeros((SUB, LANES), F32)
        row = iota((SUB, LANES), 0)
        for r in range(SUB):
            if start + r < len(values) and values[start + r] is not None:
                tile = jnp.where(row == r, values[start + r], tile)
        tiles.append(tile)
    return jnp.concatenate(tiles, 0)


def pack_kernel(
    offs_hbm, kern_hbm, pat_hbm, orbs_hbm, v_hbm, out, v_out, offs, kern, pat, orb, sems
):
    core = lax.axis_index("bricks")
    copies = [
        pltpu.make_async_copy(src, dst, sems.at[n])
        for n, (src, dst) in enumerate(
            (
                (offs_hbm, offs),
                (kern_hbm, kern),
                (pat_hbm, pat),
                (orbs_hbm.at[core], orb),
                (v_hbm, v_out),
            )
        )
    ]
    for copy in copies:
        copy.start()
    count, side = orbs_hbm.shape[0], orb.shape[0]
    groups = LANES // side
    per = side // groups
    k_at, lane = iota((side, LANES), 0), iota((side, LANES), 1)
    for copy in copies[:3]:
        copy.wait()
    table = offs[...]
    corner = [jnp.where(core == 0, table[0, axis], table[1, axis]) for axis in range(3)]
    o0, o1, o2 = corner
    turned = jnp.where((lane & (side - 1)) == ((k_at + o2) & (side - 1)), 1.0, 0.0)
    spreads = [jnp.where((lane // side) == g, turned, 0.0).astype(BF16) for g in range(groups)]
    values = [jnp.full((1, LANES), m, I32).astype(F32) for m in corner] + [None] * (SUB - 3)
    line = kern[...] * pat[...].astype(F32)
    wide = [jnp.broadcast_to(line[:, c : c + 1], (1, LANES)) for c in range(3 * count)]
    for c in range(3 * count):
        w = jnp.where(core == 0, wide[c], wide[c ^ 1])
        high = w.astype(BF16).astype(F32)
        values += [high, w - high]
    out[per] = rows_splat(values, side).astype(BF16)
    copies[3].wait()
    total = jnp.zeros((per * side, LANES), F32)
    for g in range(groups):
        planes = [orb[(g * per + i - o0) & (side - 1)] for i in range(per)]
        total = total + jnp.dot(
            jnp.concatenate(planes, 0), spreads[g], preferred_element_type=F32
        )
    for i in range(per):
        plane = pltpu.roll(total[i * side : (i + 1) * side], o1 & (side - 1), 0)
        out[i] = plane.astype(BF16)
    copies[4].wait()


def cut_window(corner, v_own, v_other, cut):
    side, depth = v_own.shape[0], v_own.shape[1]
    groups = LANES // side
    per = side // groups
    core = lax.axis_index("bricks")
    _, o1, o2 = corner
    lane = iota((side, LANES), 1)
    row = iota((side, LANES), 0)
    fold = jnp.where((lane & (side - 1)) == row, 1.0, 0.0).astype(BF16)
    folds = []
    for g in range(groups):
        block = fold * jnp.where((lane // side) == g, 1.0, 0.0).astype(BF16)
        folds += [block] * groups
    start = o2 + ((lane - o2) & (LANES - 1))
    inside = start - o2 < side
    own = inside & ((start // LANES) == core)
    other = inside & ((start // LANES) != core)
    high, left, right = [
        jnp.where(m, 1.0, 0.0).astype(BF16) > 0 for m in (row < o1, own, other)
    ]
    zero = jnp.zeros((side, LANES), BF16)
    parts = []
    for g in range(groups):
        planes = []
        for x in range(g * per, (g + 1) * per):
            one, two = [
                jnp.where(high, v[x, depth - side :].astype(BF16), v[x, 0:side].astype(BF16))
                for v in (v_own, v_other)
            ]
            planes.append(jnp.where(left, one, jnp.where(right, two, zero)))
        parts.append(jnp.concatenate(planes, 0))
    out = jnp.dot(
        jnp.concatenate(parts, 1), jnp.concatenate(folds, 0), preferred_element_type=F32
    )
    cut[...] = out.astype(BF16).reshape(per, side, LANES)


def cut_prev_kernel(offs_prev, v_own, v_other, cut):
    core = lax.axis_index("bricks")
    line = jnp.where(core == 0, offs_prev[0:1, :], offs_prev[1:2, :])
    corner = [jnp.broadcast_to(line[:, axis : axis + 1], (1, LANES)) for axis in range(3)]
    cut_window(corner, v_own, v_other, cut)


def cut_own_kernel(packet, v_own, v_other, cut):
    meta = packet[packet.shape[0] - 1].astype(F32)
    corner = [meta[axis : axis + 1].astype(I32) for axis in range(3)]
    cut_window(corner, v_own, v_other, cut)


class Tables:
    def __init__(self, packets, places):
        self.places = places
        self.metas = [packet[packet.shape[0] - 1].astype(F32) for packet in packets]
        self.corner = [
            [meta[axis : axis + 1].astype(I32) for axis in range(3)] for meta in self.metas
        ]

    def weight(self, a, b):
        (da, oa), (db, ob) = self.places[a], self.places[b]
        at = SUB + 2 * ((db - da + 1) * 2 + (oa ^ ob))
        return self.metas[a][at : at + 1] + self.metas[a][at + 1 : at + 2]

    def pair(self, a, b):
        return self.weight(a, b) if a == b else self.weight(a, b) + self.weight(b, a)


def fill_brick(prev0, prev1, own0, own1, dens, ready, placed):
    core = lax.axis_index("bricks")
    side = dens.shape[0]
    groups = LANES // side
    per = side // groups
    packets = (prev0, prev1, own0, own1)
    many = len(packets)
    tables = Tables(packets, ((0, 0), (0, 1), (1, 0), (1, 1)))
    lane = iota((1, LANES), 1)
    k_at = lane & (side - 1)
    row = iota((side, LANES), 0)
    uppers = [row < tables.corner[b][1] for b in range(many)]
    z_at = [o2 + ((k_at - o2) & (side - 1)) for _, _, o2 in tables.corner]
    links = {}
    for a in range(many):
        for b in range(a, many):
            w = tables.pair(a, b)
            if a != b:
                w = jnp.where(uppers[a] == uppers[b], jnp.where(z_at[a] == z_at[b], w, 0.0), 0.0)
            links[a, b] = jnp.broadcast_to(w, (side, LANES))
    for i in range(per):
        x = (lane // side) * per + i
        fields = []
        for b in range(many):
            o0 = tables.corner[b][0]
            keep = (x < o0) if b < 2 else (x >= o0)
            kept = packets[b][i] * jnp.where(keep, 1.0, 0.0).astype(BF16)
            fields.append(kept.astype(F32))
        for a in range(many):
            inner = links[a, a] * fields[a]
            for b in range(a + 1, many):
                inner = inner + links[a, b] * fields[b]
            product = fields[a] * inner
            high = product.astype(BF16)
            ready[a, i * side : (i + 1) * side, 0:LANES] = high
            ready[a, i * side : (i + 1) * side, LANES:] = (product - high.astype(F32)).astype(BF16)
    from_lane = iota((side, LANES), 0)
    fold = jnp.where(from_lane == (iota((side, LANES), 1) & (side - 1)), 1.0, 0.0)
    empty = jnp.zeros((side, LANES), BF16)
    for a in range(many):
        inside = z_at[a] == core * LANES + lane
        block = jnp.where(inside, fold, 0.0).astype(BF16)
        place = jnp.concatenate(
            [
                jnp.concatenate([block if h == g else empty for h in range(groups)], 1)
                for g in range(groups)
            ]
            * 2,
            0,
        )
        placed[a] = jnp.dot(ready[a], place, preferred_element_type=F32)
    for g in range(groups):
        for i in range(per):
            x = g * per + i
            parts = [placed[a, i * side : (i + 1) * side, g * LANES : (g + 1) * LANES] for a in range(many)]
            low, high = None, None
            for a in range(many):
                down = jnp.where(uppers[a], 0.0, parts[a])
                up = jnp.where(uppers[a], parts[a], 0.0)
                low = down if low is None else low + down
                high = up if high is None else high + up
            dens[x, 0:side] = low
            dens[x, side : 2 * side] = high


def mid_kernel(
    prev0, prev1, own0, own1, next0, next1, dens, mixed, bend, ready, placed
):
    side, per = own0.shape[1], own0.shape[0] - 1
    fill_brick(prev0, prev1, own0, own1, dens, ready, placed)
    packets = (prev0, prev1, own0, own1, next0, next1)
    tables = Tables(packets, ((0, 0), (0, 1), (1, 0), (1, 1), (2, 0), (2, 1)))
    me, mate = 2, 3
    lane = iota((1, LANES), 1)
    k_at = lane & (side - 1)
    row = iota((side, LANES), 0)
    a0, a1, a2 = tables.corner[me]
    z_me = a2 + ((k_at - a2) & (side - 1))
    upper = row < a1

    def same_yz(b):
        _, o1, o2 = tables.corner[b]
        z = jnp.where(o2 + ((k_at - o2) & (side - 1)) == z_me, 1.0, 0.0)
        return jnp.where((row < o1) == upper, z, 0.0)

    overlap = [None if b == me else same_yz(b) for b in range(6)]
    inner_ids, last_ids = (0, 1, me, mate), (4, 5, me, mate)
    pair = {}
    for a in range(4):
        for b in range(a, 4):
            pair[a, b] = (
                tables.pair(inner_ids[a], inner_ids[b]), tables.pair(last_ids[a], last_ids[b])
            )
    mine = [(tables.weight(me, inner_ids[b]), tables.weight(me, last_ids[b])) for b in range(4)]
    for i in range(per):
        x = (lane // side) * per + i
        spill = x < a0

        def pick(both, a, b):
            return both[0] if a >= 2 and b >= 2 else jnp.where(spill, both[1], both[0])

        fields = []
        for o in (0, 1):
            before = jnp.where((x < tables.corner[o][0]) & ~spill, 1.0, 0.0).astype(BF16)
            after = jnp.where((x >= tables.corner[4 + o][0]) & spill, 1.0, 0.0).astype(BF16)
            fields.append(
                (packets[o][i] * before).astype(F32) * overlap[o]
                + (packets[4 + o][i] * after).astype(F32) * overlap[4 + o]
            )
        fields.append(packets[me][i].astype(F32))
        also = jnp.where((x < tables.corner[mate][0]) == spill, 1.0, 0.0).astype(BF16)
        fields.append((packets[mate][i] * also).astype(F32) * overlap[mate])
        rho = None
        for a in range(4):
            inner = None
            for b in range(a, 4):
                term = pick(pair[a, b], a, b) * fields[b]
                inner = term if inner is None else inner + term
            rho = fields[a] * inner if rho is None else rho + fields[a] * inner
        mix = None
        for b in range(4):
            term = pick(mine[b], b, me) * fields[b]
            mix = term if mix is None else mix + term
        mixed[i] = mix
        bend[i] = rho * lax.rsqrt(1.0 + rho * rho)


def last_kernel(own, cut_own, cut_next, mixed, bend, dens, dens_hbm, out_hbm, out, sems):
    copies = [
        pltpu.make_async_copy(dens, dens_hbm, sems.at[0]),
        pltpu.make_async_copy(out, out_hbm, sems.at[1]),
    ]
    copies[0].start()
    side = out.shape[1]
    groups = LANES // side
    per = side // groups
    corner = own[per, 0:SUB].astype(F32).astype(I32)
    s0, s1, s2 = [corner[axis, 0] for axis in range(3)]
    lane = iota((1, LANES), 1)
    planes = []
    for i in range(per):
        spill = (lane // side) * per + i < s0
        outer = jnp.where(spill, cut_next[i].astype(F32), cut_own[i].astype(F32))
        potential = (outer + bend[i]).astype(BF16).astype(F32)
        grad = 2.0 * potential * mixed[i]
        planes.append(pltpu.roll(grad, (side - s1) & (side - 1), 0).astype(BF16))
    stacked = jnp.concatenate(planes, 0)
    from_lane, to = iota((LANES, side), 0), iota((LANES, side), 1)
    turned = (from_lane & (side - 1)) == ((to + s2) & (side - 1))
    for g in range(groups):
        gather = jnp.where(turned & ((from_lane // side) == g), 1.0, 0.0).astype(BF16)
        part = jnp.dot(stacked, gather, preferred_element_type=F32).astype(BF16)
        for i in range(per):
            out[0, (g * per + i - s0) & (side - 1)] = part[i * side : (i + 1) * side]
    copies[1].start()
    for copy in copies:
        copy.wait()


def call(kernel, outs, out_specs, ins, args, scratch, moved=2000000):
    return pl.pallas_call(
        kernel,
        out_shape=outs,
        in_specs=ins,
        out_specs=out_specs,
        scratch_shapes=scratch,
        compiler_params=pltpu.CompilerParams(vmem_limit_bytes=GRANT),
        cost_estimate=pl.CostEstimate(
            flops=1000000, bytes_accessed=moved, transcendentals=0
        ),
    )(*[
        pltpu.with_memory_space_constraint(x, pltpu.HBM) if spec is HBM else x
        for x, spec in zip(args, ins)
    ])


def step(orbitals, offsets, kernel, pattern, local_potential):
    devices = lax.axis_size("atoms")
    up = [(i, (i + 1) % devices) for i in range(devices)]
    down = [(j, i) for i, j in up]
    swap = [(0, 1), (1, 0)]
    count, side = orbitals.shape[0], orbitals.shape[1]
    depth, width = local_potential.shape[1], local_potential.shape[2]
    groups = LANES // side
    per = side // groups
    shape = jax.ShapeDtypeStruct
    dma = pltpu.SemaphoreType.DMA
    offsets_prev = lax.ppermute(offsets, "atoms", up)
    own, mine = call(
        pack_kernel,
        (shape((per + 1, side, LANES), BF16), shape(local_potential.shape, F32)),
        (VMEM,) * 2,
        [HBM] * 5,
        (offsets, kernel, pattern, orbitals, local_potential),
        [
            pltpu.VMEM(offsets.shape, I32),
            pltpu.VMEM(kernel.shape, F32),
            pltpu.VMEM(pattern.shape, I32),
            pltpu.VMEM(orbitals.shape[1:], BF16),
            dma((5,)),
        ],
    )
    prev = lax.ppermute(own, "atoms", up)
    following = lax.ppermute(own, "atoms", down)
    other = lax.ppermute(local_potential, "bricks", swap)
    own_mate = lax.ppermute(own, "bricks", swap)
    cut_prev = call(
        cut_prev_kernel,
        shape((per, side, LANES), BF16),
        VMEM,
        [VMEM] * 3,
        (offsets_prev, mine, other),
        [],
    )
    cut_next = lax.ppermute(cut_prev, "atoms", down)
    cut_own = call(
        cut_own_kernel, shape((per, side, LANES), BF16), VMEM, [VMEM] * 3, (own, mine, other), []
    )
    prev_mate = lax.ppermute(prev, "bricks", swap)
    following_mate = lax.ppermute(following, "bricks", swap)
    dens, mixed, bend = call(
        mid_kernel,
        (shape((side, depth, width), F32),) + (shape((per, side, LANES), F32),) * 2,
        (VMEM,) * 3,
        [VMEM] * 6,
        (prev, prev_mate, own, own_mate, following, following_mate),
        [
            pltpu.VMEM((2 * count, per * side, 2 * LANES), BF16),
            pltpu.VMEM((2 * count, per * side, groups * LANES), F32),
        ],
    )
    density, gradient = call(
        last_kernel,
        (shape((side, depth, width), F32), shape((1, side, side, side), BF16)),
        (HBM,) * 2,
        [VMEM] * 6,
        (own, cut_own, cut_next, mixed, bend, dens),
        [pltpu.VMEM((1, side, side, side), BF16), dma((2,))],
    )
    return density, gradient


def solution(mesh):
    return jax.shard_map(
        step,
        mesh=mesh,
        in_specs=(
            P("atoms", None, None, None),
            P("atoms", None),
            P(("atoms", "bricks"), None),
            P(("atoms", "bricks"), None),
            P("atoms", None, "bricks"),
        ),
        out_specs=(P("atoms", None, "bricks"), P(("atoms", "bricks"), None, None, None)),
        check_vma=False,
    )
```
